32 devices in a mesh: row: 4 (over x, core), col: 8 (over z, y).
Axes of the slice: x: 2, y: 2, z: 4, core: 2. Of those that a mesh axis runs over, the one named last changes fastest.
Arguments:
- coords: float32 [4, 4096], P(None, ('row', 'col')), may hold values from 0 to 1, as said below
- values: float32 [512, 4096], P(None, ('row', 'col')), may hold values from -6 to 6
- coarse_coords: float32 [4, 512], P(None, ('row', 'col')), may hold values from 0 to 1, as said below
- coarse_values: float32 [512, 512], P(None, ('row', 'col')), may hold values from -6 to 6
- fine_index: int32 [32, 128], P(('row', 'col')), may hold values from 0 to 127, as said below
- coarse_index: int32 [32, 384], P(('row', 'col')), may hold values from 0 to 511, as said below
- log_params: float32 [6], replicated, may hold values from -0.5 to 0.5
Outputs:
- step: float32 [6], replicated
- whitened: float32 [512, 4096], P(None, ('row', 'col'))
The draws below stay inside these ranges and needn't reach their ends.
Inputs may be any that keep to these rules, and one draw needn't show every extreme that they name: `fine_index`: in each row the first 64 entries are distinct, and so are the last 64. `coarse_index`: the entries of each row are distinct; in each row at most 16 entries lie in one tile (j // 16), and some tile holds exactly 16 of them. `coarse_coords`: coarse point j lies in tile j // 16; for tile (r, c) its longitude lies in [c / 8, (c + 1) / 8) and its latitude in [r / 4, (r + 1) / 4), elevation and time in [0, 1). `coords`: fine point p lies in tile p // 128, placed as for the coarse points.
All inputs are finite; a program needn't handle non-finite values.
Results may differ from the reference program's by a relative error of at most 0.0003.
Values sent between devices are 32-bit elements; how exact they have to be, the bound alone decides.
A program may use at most 192 MiB of HBM per device.

```python
import math
import jax
import jax.numpy as jnp
from jax import lax

R = 512
B = 128
FH = 64
COARSE = 384
CP = 16
TOTAL = 4096
CTOTAL = 512
N_ROW = 4
N_COL = 8
DEVICES = 32


def placed_coords(key, per_tile):
    count = DEVICES * per_tile
    unit = jax.random.uniform(key, (4, count), jnp.float32)
    owner = jnp.arange(count, dtype=jnp.int32) // per_tile
    col_pos = (owner % N_COL).astype(jnp.float32)
    row_pos = (owner // N_COL).astype(jnp.float32)
    longitude = (col_pos + unit[0]) / float(N_COL)
    latitude = (row_pos + unit[1]) / float(N_ROW)
    return jnp.stack([longitude, latitude, unit[2], unit[3]])


def draw_coords(key, part):
    return placed_coords(jax.random.fold_in(key, 11), B)


def draw_coarse_coords(key, part):
    return placed_coords(jax.random.fold_in(key, 13), CP)


def draw_fine_index(key, part):
    keys = jax.random.split(jax.random.fold_in(key, 17), 2 * DEVICES)
    picks = jax.vmap(lambda each: jax.random.permutation(each, B)[:FH])(keys)
    return picks.reshape(DEVICES, 2 * FH).astype(jnp.int32)


def one_coarse_row(each):
    limit = min(CP, 2 * ((COARSE + DEVICES - 1) // DEVICES))
    first_key, second_key, third_key = jax.random.split(each, 3)
    forced = jax.random.randint(first_key, (), 0, DEVICES, dtype=jnp.int32)
    pairs = DEVICES * limit
    ranks = jax.random.permutation(second_key, pairs).astype(jnp.int32)
    tile_of = jnp.arange(pairs, dtype=jnp.int32) // limit
    scores = jnp.where(tile_of == forced, ranks - pairs, ranks)
    chosen = jnp.argsort(scores, stable=True)[:COARSE].astype(jnp.int32)
    chosen_tile = chosen // limit
    chosen_slot = chosen % limit
    sub_keys = jax.random.split(third_key, DEVICES)
    inner = jax.vmap(lambda sub: jax.random.permutation(sub, CP))(sub_keys).astype(jnp.int32)
    return chosen_tile * CP + inner[chosen_tile, chosen_slot]


def draw_coarse_index(key, part):
    keys = jax.random.split(jax.random.fold_in(key, 19), DEVICES)
    return jax.vmap(one_coarse_row)(keys).astype(jnp.int32)


def block_scale(rng, dims, pieces, low, top_value):
    def one(dim, blocks):
        steps = jax.random.uniform(jax.random.fold_in(jax.random.fold_in(rng, 6), dim), (blocks,), jnp.float32, low / len(pieces), top_value / len(pieces))
        return jnp.repeat(jnp.exp(steps), dims[dim] // blocks).reshape((-1,) + (1,) * (len(dims) - dim - 1))

    level = one(*pieces[0])
    for cut in pieces[1:]:
        level = level * one(*cut)
    return level


def normal_values(key, shape, deviation, bound, pieces=(), kind=jnp.bfloat16):
    values = deviation * jax.random.normal(key, shape, jnp.float32)
    if pieces:
        values = values * block_scale(key, shape, pieces, -0.22, 0.18)
    return jnp.clip(values, -bound, bound).astype(kind)


def setup_inputs(seed: int = 0) -> dict:
    key_of = jax.random.split(jax.random.key(seed), 8)
    coords = draw_coords(jax.random.fold_in(key_of[7], 71), 0)
    values = normal_values(key_of[1], (R, TOTAL), 1.0, 6.0, ((1, 32),), jnp.float32)
    coarse_coords = draw_coarse_coords(jax.random.fold_in(key_of[7], 71), 0)
    coarse_values = normal_values(key_of[3], (R, CTOTAL), 1.0, 6.0, ((1, 32),), jnp.float32)
    fine_index = draw_fine_index(jax.random.fold_in(key_of[7], 71), 0)
    coarse_index = draw_coarse_index(jax.random.fold_in(key_of[7], 71), 0)
    log_params = jnp.clip(jax.random.uniform(key_of[6], (6,), jnp.float32, -0.5, 0.5), -0.5, 0.5)
    return dict(coords=coords, values=values, coarse_coords=coarse_coords, coarse_values=coarse_values, fine_index=fine_index, coarse_index=coarse_index, log_params=log_params)


HIGH = lax.Precision.HIGHEST
ROOT_FIVE = math.sqrt(5.0)
NUGGET = 0.2
RANGE_BASE = (0.5, 0.5, 0.5, 0.5)

def local_covariance(joint_coords, live, theta):
    count = joint_coords.shape[1]
    scale = jnp.exp(theta[1:5]) * jnp.array(RANGE_BASE)
    scaled = joint_coords / scale[:, None]
    diff = scaled[:, :, None] - scaled[:, None, :]
    squares = diff * diff
    dist = jnp.sqrt(lax.optimization_barrier(jnp.sum(squares, axis=0)))
    root = ROOT_FIVE * dist
    decay = jnp.exp(-root)
    variance = jnp.exp(theta[0])
    kernel = variance * (1.0 + root + root * root / 3.0) * decay
    common = variance * (5.0 / 3.0) * (1.0 + root) * decay
    paired = live[:, None] * live[None, :]
    ident = jnp.eye(count, dtype=jnp.float32)
    nugget = NUGGET * jnp.exp(theta[5])
    cov = paired * kernel + (live * nugget + 1.0 - live)[:, None] * ident
    derivs = jnp.concatenate([(paired * kernel)[None], (paired * common)[None] * squares, ((live * nugget)[:, None] * ident)[None]], axis=0)
    return (cov, derivs)

def fisher_terms(cov, derivs, lead, reps):
    count = cov.shape[0]
    ident = jnp.eye(count, dtype=jnp.float32)
    factor = jnp.linalg.cholesky(cov)
    inverse = jax.scipy.linalg.solve_triangular(factor, ident, lower=True)
    joint_prec = jnp.dot(inverse.T, inverse, precision=HIGH)
    lead_inv = inverse[:lead, :lead]
    lead_prec = jnp.dot(lead_inv.T, lead_inv, precision=HIGH)
    joint_prod = jnp.einsum('ab,ibc->iac', joint_prec, derivs, precision=HIGH)
    lead_prod = jnp.einsum('ab,ibc->iac', lead_prec, derivs[:, :lead, :lead], precision=HIGH)
    joint_fish = jnp.einsum('iab,jba->ij', joint_prod, joint_prod, precision=HIGH)
    lead_fish = jnp.einsum('iab,jba->ij', lead_prod, lead_prod, precision=HIGH)
    fisher = reps * 0.5 * (joint_fish - lead_fish)
    traces = jnp.trace(joint_prod, axis1=1, axis2=2) - jnp.trace(lead_prod, axis1=1, axis2=2)
    return (inverse, fisher, traces)

def score_terms(inverse, derivs, joint_values, traces, lead, reps):
    white = jnp.dot(joint_values, inverse.T, precision=HIGH)
    alpha = jnp.dot(white, inverse, precision=HIGH)
    lead_alpha = jnp.dot(white[:, :lead], inverse[:lead, :lead], precision=HIGH)
    joint_quad = lax.optimization_barrier(jnp.sum(jnp.einsum('rn,inm->irm', alpha, derivs, precision=HIGH) * alpha[None], axis=(1, 2)))
    lead_quad = lax.optimization_barrier(jnp.sum(jnp.einsum('rn,inm->irm', lead_alpha, derivs[:, :lead, :lead], precision=HIGH) * lead_alpha[None], axis=(1, 2)))
    grad = 0.5 * (joint_quad - lead_quad) - 0.5 * reps * traces
    return (grad, white[:, lead:])

def reference(coords, values, coarse_coords, coarse_values, fine_index, coarse_index, log_params):
    lead = COARSE + 2 * FH
    tile_coords = coords.reshape(4, DEVICES, B)
    tile_values = values.reshape(R, DEVICES, B)

    def one_block(device):
        row_pos = device // N_COL
        col_pos = device % N_COL
        upper = jnp.maximum(device - N_COL, 0).astype(jnp.int32)
        left = (row_pos * N_COL + (col_pos + N_COL - 1) % N_COL).astype(jnp.int32)
        upper_live = (row_pos > 0).astype(jnp.float32)
        picks = fine_index[device]
        wanted = coarse_index[device]
        upper_coords = jnp.take(jnp.take(tile_coords, upper, axis=1), picks[:FH], axis=1) * upper_live
        upper_values = jnp.take(jnp.take(tile_values, upper, axis=1), picks[:FH], axis=1) * upper_live
        left_coords = jnp.take(jnp.take(tile_coords, left, axis=1), picks[FH:], axis=1)
        left_values = jnp.take(jnp.take(tile_values, left, axis=1), picks[FH:], axis=1)
        joint_coords = jnp.concatenate([jnp.take(coarse_coords, wanted, axis=1), upper_coords, left_coords, jnp.take(tile_coords, device, axis=1)], axis=1)
        joint_values = jnp.concatenate([jnp.take(coarse_values, wanted, axis=1), upper_values, left_values, jnp.take(tile_values, device, axis=1)], axis=1)
        live = jnp.concatenate([jnp.ones((COARSE,), jnp.float32), upper_live * jnp.ones((FH,), jnp.float32), jnp.ones((FH + B,), jnp.float32)])
        cov, derivs = local_covariance(joint_coords, live, log_params)
        inverse, fisher, traces = fisher_terms(cov, derivs, lead, R)
        grad, white = score_terms(inverse, derivs, joint_values, traces, lead, R)
        return (grad, fisher, white)
    grads, fishers, whites = lax.map(one_block, jnp.arange(DEVICES, dtype=jnp.int32))
    grad = lax.optimization_barrier(jnp.sum(grads, axis=0))
    fisher = lax.optimization_barrier(jnp.sum(fishers, axis=0))
    step = jax.scipy.linalg.cho_solve((jnp.linalg.cholesky(fisher), True), grad)
    whitened = jnp.transpose(whites, (1, 0, 2)).reshape(R, DEVICES * B)
    return (step, whitened)
```

```python
import functools
import math

import jax
import jax.numpy as jnp
from jax import lax
from jax.experimental import pallas as pl
from jax.experimental.pallas import tpu as pltpu
from jax.sharding import PartitionSpec as P

HIGH = lax.Precision.HIGHEST
ROOT_FIVE = math.sqrt(5.0)
NUGGET = 0.2
RANGE_BASE = (0.5, 0.5, 0.5, 0.5)
BLK = 128
PAN = 16
F32 = jnp.float32


def mm(a, b):
    return jnp.dot(a, b, precision=HIGH, preferred_element_type=F32)


def mm_tn(a, b):
    return lax.dot_general(
        a, b, (((0,), (0,)), ((), ())), precision=HIGH, preferred_element_type=F32
    )


def halves(x):
    high = x.astype(jnp.bfloat16)
    return high, (x - high.astype(F32)).astype(jnp.bfloat16)


def split_dot(a, b, dims):
    def dot(x, y):
        return lax.dot_general(x, y, (dims, ((), ())), preferred_element_type=F32)

    (ah, al), (bh, bl) = a, b
    return dot(ah, bh) + (dot(ah, bl) + dot(al, bh))


def mm3(a, b):
    return split_dot(halves(a), halves(b), ((1,), (0,)))


def mm3_tn(a, b):
    return split_dot(halves(a), halves(b), ((0,), (0,)))


def rows(b):
    return pl.ds(b * BLK, BLK)


def inverse_factor(s_ref):
    row = lax.broadcasted_iota(jnp.int32, (PAN, BLK), 0)
    lane = lax.broadcasted_iota(jnp.int32, (PAN, BLK), 1)

    def panel(p, carry):
        start = pl.multiple_of(p * PAN, PAN)
        xa = s_ref[pl.ds(start, PAN), :BLK]
        xb = s_ref[pl.ds(start, PAN), BLK:]
        turned = pltpu.roll(xa, lax.rem(BLK - start, BLK), 1)
        cols = [jnp.broadcast_to(turned[:, j : j + 1], (PAN, BLK)) for j in range(PAN)]
        for k in range(PAN):
            inv = lax.rsqrt(cols[k][k : k + 1, :])
            low = cols[k] * inv
            for j in range(k + 1, PAN):
                cols[j] = cols[j] - low * low[j : j + 1, :]
            below = jnp.where(row > k, low, 0.0)
            ua = xa[k : k + 1, :] * inv
            ub = xb[k : k + 1, :] * inv
            xa = jnp.where(row == k, ua, xa - below * ua)
            xb = jnp.where(row == k, ub, xb - below * ub)
        s_ref[pl.ds(start, PAN), :BLK] = xa
        s_ref[pl.ds(start, PAN), BLK:] = xb
        tail = jnp.where(lane >= start + PAN, xa, 0.0)
        s_ref[...] -= mm_tn(tail, jnp.concatenate([xa, xb], axis=1))
        return carry

    lax.fori_loop(0, BLK // PAN, panel, 0)


def forward(u_ref, inv_ref, x_ref, count):
    for b in range(count):
        part = x_ref[rows(b), :]
        if b:
            part = part - mm3_tn(u_ref[: b * BLK, b * BLK : (b + 1) * BLK], x_ref[: b * BLK, :])
        x_ref[rows(b), :] = mm3(inv_ref[rows(b), :], part)


MESH = pl.DeviceIdType.MESH


def onehot(index, count):
    return (lax.broadcasted_iota(jnp.int32, (count, index.shape[1]), 0) == index).astype(F32)


def fused_kernel(
    per_tile, lp, coords, ccoords, cidx, fidx, values, coarse, step_ref, white_ref,
    u_ref, inv_ref, wt_ref, h_ref, z_ref, c_ref, s_ref, xr, xc, m_ref, pay, near, ccv, ccrow, ccrows,
    cbuf, fbuf, own, upper, left, allc, term, terms, local_sem, send_sem, recv_sem,
):
    n_row, n_col = lax.axis_size("row"), lax.axis_size("col")
    count = n_row * n_col
    row, col = lax.axis_index("row"), lax.axis_index("col")
    me = row * n_col + col
    reps = values.shape[0]
    n = xr.shape[1]
    nb = n // BLK
    lead = n - BLK
    lb = nb - 1
    nc = cidx.shape[1]
    half = fidx.shape[1] // 2

    def place(d):
        other = lax.rem(me + d, count)
        return {"row": other // n_col, "col": lax.rem(other, n_col)}

    barrier = pltpu.get_barrier_semaphore()

    def greet(d, carry):
        pl.semaphore_signal(barrier, inc=1, device_id=place(d), device_id_type=MESH)
        return carry

    def fetch(src, dst, k):
        return pltpu.make_async_copy(src, dst, local_sem.at[k])

    early = [
        fetch(coords, pay.at[pl.ds(0, 4)], 0), fetch(ccoords, ccv, 1),
        fetch(cidx, cbuf, 2), fetch(fidx, fbuf, 3),
    ]
    late = [
        fetch(values, own, 4), fetch(coarse, allc.at[pl.ds(me * per_tile, per_tile)], 5),
    ]
    for each in early:
        each.start()
    lax.fori_loop(1, count, greet, 0)
    pay[4:, :] = jnp.zeros((4, BLK), F32)
    early[0].wait()
    early[1].wait()
    small = ccv[...]
    line = jnp.zeros((1, BLK), F32)
    wide = jnp.concatenate([small, jnp.zeros((4, BLK - per_tile), F32)], axis=1)
    for k in range(4):
        part = wide[k : k + 1, :]
        line = line + (pltpu.roll(part, k * per_tile, 1) if k else part)
    ccrow[...] = line
    ccrows[pl.ds(me, 1), :] = line
    pl.semaphore_wait(barrier, count - 1)

    def send(src, dst, k, where):
        return pltpu.make_async_remote_copy(
            src_ref=src, dst_ref=dst, send_sem=send_sem.at[k], recv_sem=recv_sem.at[k],
            device_id=where, device_id_type=MESH,
        )

    def push(src, dst, k):
        def step(d, carry):
            send(src, dst, k, place(d)).start()
            return carry

        lax.fori_loop(1, count, step, 0)

    def landed(ref, k):
        pltpu.make_async_copy(ref, ref, recv_sem.at[k]).wait()

    def left_here(ref, k):
        pltpu.make_async_copy(ref, ref, send_sem.at[k]).wait()

    down = {"row": lax.rem(row + 1, n_row)}
    across = {"col": lax.rem(col + 1, n_col)}
    push(ccrow, ccrows.at[pl.ds(me, 1)], 0)
    near_down = send(pay, near.at[0], 1, down)
    near_across = send(pay, near.at[1], 2, across)
    near_down.start()
    near_across.start()
    for each in late:
        each.start()
    field_down = send(values, upper, 3, down)
    field_across = send(values, left, 4, across)
    field_down.start()
    field_across.start()
    push(coarse, allc.at[pl.ds(me * per_tile, per_tile)], 5)

    row8 = lax.broadcasted_iota(jnp.int32, (8, BLK), 0)
    spread = jnp.zeros((8, BLK), F32)
    for k in range(4):
        spread = jnp.where(row8 == k, lp[1 + k], spread)
    base = jnp.ones((8, BLK), F32)
    for k in range(4):
        base = jnp.where(row8 == k, RANGE_BASE[k], base)
    scale = (1.0 / (jnp.exp(spread) * base))[:, :1]
    variance = jnp.exp(jnp.full((1, BLK), lp[0], F32))[:, :1]
    nugget = (NUGGET * jnp.exp(jnp.full((1, BLK), lp[5], F32)))[:, :1]
    alive = jnp.where(row > 0, 1.0, 0.0)

    early[2].wait()
    early[3].wait()
    wanted = cbuf[...]
    tile = wanted // per_tile
    slot = wanted - tile * per_tile
    hot_t = onehot(tile, count)
    hot_s = onehot(slot, per_tile)
    pick_u = onehot(fbuf[:, :half], BLK)
    pick_l = onehot(fbuf[:, half:], BLK)

    near_down.wait_recv()
    near_across.wait_recv()
    xr[:, nc : nc + half] = mm(near[0], pick_u) * (scale * alive)
    xr[:, nc + half : lead] = mm(near[1], pick_l) * scale
    xr[:, lead:] = pay[...] * scale
    landed(ccrows.at[pl.ds(0, count - 1)], 0)
    lines = mm_tn(ccrows[...], hot_t)
    for k in range(4):
        part = lines[k * per_tile : (k + 1) * per_tile, :] * hot_s
        xr[k : k + 1, :nc] = jnp.sum(part, axis=0, keepdims=True) * scale[k : k + 1, :]
    xr[5:, :nc] = jnp.zeros((3, nc), F32)
    point = lax.broadcasted_iota(jnp.int32, (1, n), 1)
    xr[4:5, :] = jnp.where((point >= nc) & (point < nc + half), alive, 1.0)
    for b in range(nb):
        xc[rows(b), :] = xr[:, b * BLK : (b + 1) * BLK].T

    def cover(r, carry):
        start = pl.multiple_of(r * 64, 64)
        here = pl.ds(start, 64)
        total = None
        for k in range(4):
            diff = xc[here, k : k + 1] - xr[k : k + 1, :]
            total = diff * diff if total is None else total + diff * diff
        live_c = xc[here, 4:5]
        paired = live_c * xr[4:5, :]
        root = ROOT_FIVE * jnp.sqrt(total)
        decay = jnp.exp(-root) * (variance * paired)
        ident = (
            lax.broadcasted_iota(jnp.int32, (64, n), 0) + start
            == lax.broadcasted_iota(jnp.int32, (64, n), 1)
        )
        u_ref[here, :] = (1.0 + root + root * root / 3.0) * decay + jnp.where(
            ident, live_c * nugget + 1.0 - live_c, 0.0
        )
        c_ref[here, :] = (5.0 / 3.0) * (1.0 + root) * decay
        return carry

    lax.fori_loop(0, n // 64, cover, 0)

    eye = (
        lax.broadcasted_iota(jnp.int32, (BLK, BLK), 0)
        == lax.broadcasted_iota(jnp.int32, (BLK, BLK), 1)
    ).astype(F32)
    for b in range(nb):
        s_ref[:, :BLK] = u_ref[rows(b), b * BLK : (b + 1) * BLK]
        s_ref[:, BLK:] = eye
        inverse_factor(s_ref)
        inv = s_ref[:, BLK:]
        inv_ref[rows(b), :] = inv
        if b + 1 < nb:
            rest = (b + 1) * BLK
            u_ref[rows(b), rest:] = mm(inv, u_ref[rows(b), rest:])
            for i in range(b + 1, nb):
                u_ref[rows(i), i * BLK :] -= mm_tn(
                    u_ref[rows(b), i * BLK : (i + 1) * BLK], u_ref[rows(b), i * BLK :]
                )

    last = inv_ref[rows(lb), :]
    wt_ref[rows(lb), :] = last.T
    right = -mm(u_ref[:lead, lead:], last.T)
    for b in range(lb - 1, -1, -1):
        part = right[b * BLK : (b + 1) * BLK, :]
        if b + 1 < lb:
            part = part - mm(u_ref[rows(b), (b + 1) * BLK : lead], wt_ref[(b + 1) * BLK : lead, :])
        wt_ref[rows(b), :] = mm_tn(inv_ref[rows(b), :], part)

    wt = halves(wt_ref[...])

    def slopes(r, carry):
        here = pl.ds(pl.multiple_of(r * BLK, BLK), BLK)
        for k in range(4):
            diff = xc[here, k : k + 1] - xr[k : k + 1, :]
            h_ref[here, k * BLK : (k + 1) * BLK] = split_dot(
                halves(c_ref[here, :] * (diff * diff)), wt, ((1,), (0,))
            )
        h_ref[here, 4 * BLK :] = nugget * wt_ref[here, :]
        return carry

    lax.fori_loop(0, nb, slopes, 0)
    z_ref[...] = split_dot(wt, halves(h_ref[...]), ((0,), (0,)))
    forward(u_ref, inv_ref, h_ref, lb)

    def h_of(i):
        i = 4 if i in (0, 5) else i - 1
        return h_ref[:lead, i * BLK : (i + 1) * BLK]

    def z_of(i):
        if i == 0:
            return eye - z_ref[:, 4 * BLK :]
        return z_ref[:, (i - 1) * BLK : i * BLK]

    lane1 = lax.broadcasted_iota(jnp.int32, (1, BLK), 1)
    out = jnp.zeros((1, BLK), F32)
    spot = 0
    for i in range(6):
        for j in range(i, 6):
            sign = -2.0 if (i == 0) != (j == 0) else 2.0
            both = sign * jnp.sum(h_of(i) * h_of(j), axis=0, keepdims=True)
            both = both + jnp.sum(z_of(i) * z_of(j), axis=0, keepdims=True)
            value = (0.5 * reps) * jnp.sum(both, axis=1, keepdims=True)
            out = out + jnp.where(lane1 == spot, value, 0.0)
            spot += 1


    left_here(ccrows.at[pl.ds(0, count - 1)], 0)
    near_down.wait_send()
    near_across.wait_send()
    for each in late:
        each.wait()
    field_down.wait()
    field_across.wait()
    landed(allc.at[pl.ds(0, (count - 1) * per_tile)], 5)
    left_here(allc.at[pl.ds(0, (count - 1) * per_tile)], 5)

    hot_c = onehot(cbuf[...], count * per_tile)
    hot_u = onehot(fbuf[:, :half], BLK) * alive
    hot_l = onehot(fbuf[:, half:], BLK)
    white = mm3_tn(mm3(hot_c, wt_ref[:nc, :]), allc[...]).T
    white = white + mm3(upper[...], mm3(hot_u, wt_ref[nc : nc + half, :]))
    white = white + mm3(left[...], mm3(hot_l, wt_ref[nc + half : lead, :]))
    white = white + mm3(own[...], wt_ref[lead:, :])
    white_ref[...] = white
    m_ref[:nc, :] = mm3_tn(hot_c, mm3(allc[...], white))
    m_ref[nc : nc + half, :] = mm3_tn(hot_u, mm3_tn(upper[...], white))
    m_ref[nc + half :, :] = mm3_tn(hot_l, mm3_tn(left[...], white))
    forward(u_ref, inv_ref, m_ref, lead // BLK)
    gram = mm3_tn(white, white)
    weight = 0.5 * gram - (0.5 * reps) * eye
    for i in range(6):
        at = 4 if i in (0, 5) else i - 1
        lead_part = jnp.sum(m_ref[...] * h_ref[:lead, at * BLK : (at + 1) * BLK], axis=0, keepdims=True)
        z = z_ref[:, at * BLK : (at + 1) * BLK]
        if i == 0:
            z = eye - z
            lead_part = -lead_part
        both = lead_part + jnp.sum(weight * z, axis=0, keepdims=True)
        value = jnp.sum(both, axis=1, keepdims=True)
        out = out + jnp.where(lane1 == 21 + i, value, 0.0)

    term[...] = out
    terms[pl.ds(me, 1), :] = out
    push(term, terms.at[pl.ds(me, 1)], 6)
    landed(terms.at[pl.ds(0, count - 1)], 6)
    total = jnp.sum(terms[...], axis=0, keepdims=True)
    cell = {}
    spot = 0
    for i in range(6):
        for j in range(i, 6):
            cell[i, j] = total[:, spot : spot + 1]
            spot += 1
    right_side = [total[:, 21 + i : 22 + i] for i in range(6)]
    for k in range(6):
        inv = 1.0 / cell[k, k]
        for i in range(k + 1, 6):
            ratio = cell[k, i] * inv
            for j in range(i, 6):
                cell[i, j] = cell[i, j] - ratio * cell[k, j]
            right_side[i] = right_side[i] - ratio * right_side[k]
    for k in range(5, -1, -1):
        acc = right_side[k]
        for j in range(k + 1, 6):
            acc = acc - cell[k, j] * right_side[j]
        right_side[k] = acc / cell[k, k]
    result = jnp.zeros((1, BLK), F32)
    for i in range(6):
        result = jnp.where(lane1 == i, right_side[i], result)
    step_ref[...] = result
    left_here(terms.at[pl.ds(0, count - 1)], 6)


def shape(*dims):
    return jax.ShapeDtypeStruct(dims, F32)


def body(coords, values, coarse_coords, coarse_values, fine_index, coarse_index, log_params):
    half = fine_index.shape[1] // 2
    reps, block = values.shape
    nc = coarse_index.shape[1]
    per_tile = coarse_coords.shape[1]
    n = nc + 2 * half + block
    lead = n - block
    count = lax.axis_size("row") * lax.axis_size("col")
    anywhere = pl.BlockSpec(memory_space=pl.ANY)
    inner = pl.BlockSpec(memory_space=pltpu.VMEM)
    step, white = pl.pallas_call(
        functools.partial(fused_kernel, per_tile),
        out_shape=[shape(1, BLK), shape(reps, block)],
        in_specs=[pl.BlockSpec(memory_space=pltpu.SMEM)] + [anywhere] * 6,
        out_specs=[inner, inner],
        scratch_shapes=[
            pltpu.VMEM((n, n), F32), pltpu.VMEM((n, BLK), F32), pltpu.VMEM((n, BLK), F32),
            pltpu.VMEM((n, 5 * BLK), F32), pltpu.VMEM((BLK, 5 * BLK), F32),
            pltpu.VMEM((n, n), F32), pltpu.VMEM((BLK, 2 * BLK), F32),
            pltpu.VMEM((8, n), F32), pltpu.VMEM((n, 8), F32), pltpu.VMEM((lead, BLK), F32),
            pltpu.VMEM((8, BLK), F32), pltpu.VMEM((2, 8, BLK), F32), pltpu.VMEM((4, per_tile), F32),
            pltpu.VMEM((1, BLK), F32), pltpu.VMEM((count, BLK), F32),
            pltpu.VMEM((1, nc), jnp.int32), pltpu.VMEM((1, 2 * half), jnp.int32),
            pltpu.VMEM((reps, block), F32), pltpu.VMEM((reps, block), F32),
            pltpu.VMEM((reps, block), F32), pltpu.VMEM((count * per_tile, reps), F32),
            pltpu.VMEM((1, BLK), F32), pltpu.VMEM((count, BLK), F32),
            pltpu.SemaphoreType.DMA((6,)), pltpu.SemaphoreType.DMA((7,)),
            pltpu.SemaphoreType.DMA((7,)),
        ],
        compiler_params=pltpu.CompilerParams(
            collective_id=0, has_side_effects=True, vmem_limit_bytes=48 * 1024 * 1024
        ),
    )(log_params, coords, coarse_coords, coarse_index, fine_index, values, coarse_values.T)
    return step[0, :6], white


def solution(mesh):
    in_specs = (
        P(None, ("row", "col")),
        P(None, ("row", "col")),
        P(None, ("row", "col")),
        P(None, ("row", "col")),
        P(("row", "col"), None),
        P(("row", "col"), None),
        P(),
    )
    out_specs = (P(), P(None, ("row", "col")))
    return jax.shard_map(body, mesh=mesh, in_specs=in_specs, out_specs=out_specs, check_vma=False)
```

```python
import functools
import math

import jax
import jax.numpy as jnp
from jax import lax
from jax.experimental import pallas as pl
from jax.experimental.pallas import tpu as pltpu
from jax.sharding import PartitionSpec as P

HIGH = lax.Precision.HIGHEST
ROOT_FIVE = math.sqrt(5.0)
NUGGET = 0.2
RANGE_BASE = (0.5, 0.5, 0.5, 0.5)
BLK = 128
PAN = 16
F32 = jnp.float32


def mm(a, b):
    return jnp.dot(a, b, precision=HIGH, preferred_element_type=F32)


def mm_tn(a, b):
    return lax.dot_general(
        a, b, (((0,), (0,)), ((), ())), precision=HIGH, preferred_element_type=F32
    )


def halves(x):
    high = x.astype(jnp.bfloat16)
    return high, (x - high.astype(F32)).astype(jnp.bfloat16)


def split_dot(a, b, dims):
    def dot(x, y):
        return lax.dot_general(x, y, (dims, ((), ())), preferred_element_type=F32)

    (ah, al), (bh, bl) = a, b
    return dot(ah, bh) + (dot(ah, bl) + dot(al, bh))


def mm3(a, b):
    return split_dot(halves(a), halves(b), ((1,), (0,)))


def mm3_tn(a, b):
    return split_dot(halves(a), halves(b), ((0,), (0,)))


def rows(b):
    return pl.ds(b * BLK, BLK)


def thirds(x):
    first = x.astype(jnp.bfloat16)
    rest = x - first.astype(F32)
    second = rest.astype(jnp.bfloat16)
    return first, second, (rest - second.astype(F32)).astype(jnp.bfloat16)


def outer_tn(x):
    a, b, c = thirds(x)
    left = jnp.concatenate([a, a, b, b, a, c], axis=0)[:, :BLK]
    right = jnp.concatenate([a, b, a, b, c, a], axis=0)
    return lax.dot_general(
        left, right, (((0,), (0,)), ((), ())), preferred_element_type=F32
    )


def spread_row(x, i):
    return jnp.broadcast_to(x[i : i + 1, :], (8, BLK))


def inverse_factor(s_ref):
    row8 = lax.broadcasted_iota(jnp.int32, (8, BLK), 0)
    panels = BLK // PAN
    own = PAN // 8
    va = [s_ref[g * 8 : g * 8 + 8, :BLK] for g in range(own)]
    vb = [s_ref[g * 8 : g * 8 + 8, BLK:] for g in range(own)]
    for p in range(panels):
        base = p * PAN
        groups = 2 * own if p + 1 < panels else own
        for g in range(own, groups):
            at = base + g * 8
            va.append(s_ref[at : at + 8, :BLK])
            vb.append(s_ref[at : at + 8, BLK:])
        cols = [
            [
                jnp.broadcast_to(va[g][:, base + j : base + j + 1], (8, BLK)) if g >= j // 8 else None
                for g in range(groups)
            ]
            for j in range(PAN)
        ]
        pivots = [jnp.ones((8, BLK), F32)] * own
        for k in range(PAN):
            gk, kk = divmod(k, 8)
            pivot = spread_row(cols[k][gk], kk)
            pivots[gk] = jnp.where(row8 == kk, pivot, pivots[gk])
            inv = 1.0 / pivot
            low = [cols[k][g] * inv if g >= gk else None for g in range(groups)]
            low[gk] = jnp.where(row8 > kk, low[gk], 0.0)
            for j in range(k + 1, PAN):
                other = spread_row(cols[k][j // 8], j % 8)
                for g in range(j // 8, groups):
                    cols[j][g] = cols[j][g] - low[g] * other
            xa, xb = spread_row(va[gk], kk), spread_row(vb[gk], kk)
            for g in range(gk, groups):
                va[g] = va[g] - low[g] * xa
                vb[g] = vb[g] - low[g] * xb
        for g in range(own):
            unit = lax.rsqrt(pivots[g])
            va[g] = va[g] * unit
            vb[g] = vb[g] * unit
            s_ref[base + g * 8 : base + g * 8 + 8, BLK:] = vb[g]
        done = base + 2 * PAN
        if done < BLK:
            top = jnp.concatenate(
                [jnp.concatenate(va[:own], axis=0), jnp.concatenate(vb[:own], axis=0)], axis=1
            )
            s_ref[done:, :] -= outer_tn(top)[done:, :]
        va, vb = va[own:], vb[own:]


def forward(u_ref, inv_ref, x_ref, count):
    for b in range(count):
        part = x_ref[rows(b), :]
        if b:
            part = part - mm3_tn(u_ref[: b * BLK, b * BLK : (b + 1) * BLK], x_ref[: b * BLK, :])
        x_ref[rows(b), :] = mm3(inv_ref[rows(b), :], part)


MESH = pl.DeviceIdType.MESH


def onehot(index, count):
    return (lax.broadcasted_iota(jnp.int32, (count, index.shape[1]), 0) == index).astype(F32)


def fused_kernel(
    per_tile, lp, coords, ccoords, cidx, fidx, values, coarse, step_ref, white_ref,
    u_ref, inv_ref, wt_ref, h_ref, z_ref, c_ref, s_ref, xr, xc, m_ref, pay, near, ccv, ccrow, ccrows,
    cbuf, fbuf, own, upper, left, allc, term, terms, local_sem, send_sem, recv_sem,
):
    n_row, n_col = lax.axis_size("row"), lax.axis_size("col")
    count = n_row * n_col
    row, col = lax.axis_index("row"), lax.axis_index("col")
    me = row * n_col + col
    reps = values.shape[0]
    n = xr.shape[1]
    nb = n // BLK
    lead = n - BLK
    lb = nb - 1
    nc = cidx.shape[1]
    half = fidx.shape[1] // 2

    def place(d):
        other = lax.rem(me + d, count)
        return {"row": other // n_col, "col": lax.rem(other, n_col)}

    barrier = pltpu.get_barrier_semaphore()

    def greet(d, carry):
        pl.semaphore_signal(barrier, inc=1, device_id=place(d), device_id_type=MESH)
        return carry

    def fetch(src, dst, k):
        return pltpu.make_async_copy(src, dst, local_sem.at[k])

    early = [
        fetch(coords, pay.at[pl.ds(0, 4)], 0), fetch(ccoords, ccv, 1),
        fetch(cidx, cbuf, 2), fetch(fidx, fbuf, 3),
    ]
    late = [
        fetch(values, own, 4), fetch(coarse, allc.at[pl.ds(me * per_tile, per_tile)], 5),
    ]
    for each in early:
        each.start()
    lax.fori_loop(1, count, greet, 0)
    pay[4:, :] = jnp.zeros((4, BLK), F32)
    early[0].wait()
    early[1].wait()
    small = ccv[...]
    line = jnp.zeros((1, BLK), F32)
    wide = jnp.concatenate([small, jnp.zeros((4, BLK - per_tile), F32)], axis=1)
    for k in range(4):
        part = wide[k : k + 1, :]
        line = line + (pltpu.roll(part, k * per_tile, 1) if k else part)
    ccrow[...] = line
    ccrows[pl.ds(me, 1), :] = line
    pl.semaphore_wait(barrier, count - 1)

    def send(src, dst, k, where):
        return pltpu.make_async_remote_copy(
            src_ref=src, dst_ref=dst, send_sem=send_sem.at[k], recv_sem=recv_sem.at[k],
            device_id=where, device_id_type=MESH,
        )

    def push(src, dst, k):
        def step(d, carry):
            send(src, dst, k, place(d)).start()
            return carry

        lax.fori_loop(1, count, step, 0)

    def landed(ref, k):
        pltpu.make_async_copy(ref, ref, recv_sem.at[k]).wait()

    def left_here(ref, k):
        pltpu.make_async_copy(ref, ref, send_sem.at[k]).wait()

    down = {"row": lax.rem(row + 1, n_row)}
    across = {"col": lax.rem(col + 1, n_col)}
    push(ccrow, ccrows.at[pl.ds(me, 1)], 0)
    near_down = send(pay, near.at[0], 1, down)
    near_across = send(pay, near.at[1], 2, across)
    near_down.start()
    near_across.start()
    for each in late:
        each.start()
    field_down = send(values, upper, 3, down)
    field_across = send(values, left, 4, across)
    field_down.start()
    field_across.start()
    push(coarse, allc.at[pl.ds(me * per_tile, per_tile)], 5)

    row8 = lax.broadcasted_iota(jnp.int32, (8, BLK), 0)
    spread = jnp.zeros((8, BLK), F32)
    for k in range(4):
        spread = jnp.where(row8 == k, lp[1 + k], spread)
    base = jnp.ones((8, BLK), F32)
    for k in range(4):
        base = jnp.where(row8 == k, RANGE_BASE[k], base)
    scale = (1.0 / (jnp.exp(spread) * base))[:, :1]
    variance = jnp.exp(jnp.full((1, BLK), lp[0], F32))[:, :1]
    nugget = (NUGGET * jnp.exp(jnp.full((1, BLK), lp[5], F32)))[:, :1]
    alive = jnp.where(row > 0, 1.0, 0.0)

    early[2].wait()
    early[3].wait()
    wanted = cbuf[...]
    tile = wanted // per_tile
    slot = wanted - tile * per_tile
    hot_t = onehot(tile, count)
    hot_s = onehot(slot, per_tile)
    pick_u = onehot(fbuf[:, :half], BLK)
    pick_l = onehot(fbuf[:, half:], BLK)

    near_down.wait_recv()
    near_across.wait_recv()
    xr[:, nc : nc + half] = mm(near[0], pick_u) * (scale * alive)
    xr[:, nc + half : lead] = mm(near[1], pick_l) * scale
    xr[:, lead:] = pay[...] * scale
    landed(ccrows.at[pl.ds(0, count - 1)], 0)
    lines = mm_tn(ccrows[...], hot_t)
    for k in range(4):
        part = lines[k * per_tile : (k + 1) * per_tile, :] * hot_s
        xr[k : k + 1, :nc] = jnp.sum(part, axis=0, keepdims=True) * scale[k : k + 1, :]
    xr[5:, :nc] = jnp.zeros((3, nc), F32)
    point = lax.broadcasted_iota(jnp.int32, (1, n), 1)
    xr[4:5, :] = jnp.where((point >= nc) & (point < nc + half), alive, 1.0)
    for b in range(nb):
        xc[rows(b), :] = xr[:, b * BLK : (b + 1) * BLK].T

    def cover(r, carry):
        start = pl.multiple_of(r * 64, 64)
        here = pl.ds(start, 64)
        total = None
        for k in range(4):
            diff = xc[here, k : k + 1] - xr[k : k + 1, :]
            total = diff * diff if total is None else total + diff * diff
        live_c = xc[here, 4:5]
        paired = live_c * xr[4:5, :]
        root = ROOT_FIVE * jnp.sqrt(total)
        decay = jnp.exp(-root) * (variance * paired)
        ident = (
            lax.broadcasted_iota(jnp.int32, (64, n), 0) + start
            == lax.broadcasted_iota(jnp.int32, (64, n), 1)
        )
        u_ref[here, :] = (1.0 + root + root * root / 3.0) * decay + jnp.where(
            ident, live_c * nugget + 1.0 - live_c, 0.0
        )
        c_ref[here, :] = (5.0 / 3.0) * (1.0 + root) * decay
        return carry

    lax.fori_loop(0, n // 64, cover, 0)

    eye = (
        lax.broadcasted_iota(jnp.int32, (BLK, BLK), 0)
        == lax.broadcasted_iota(jnp.int32, (BLK, BLK), 1)
    ).astype(F32)
    for b in range(nb):
        s_ref[:, :BLK] = u_ref[rows(b), b * BLK : (b + 1) * BLK]
        s_ref[:, BLK:] = eye
        inverse_factor(s_ref)
        inv = s_ref[:, BLK:]
        inv_ref[rows(b), :] = inv
        if b + 1 < nb:
            rest = (b + 1) * BLK
            u_ref[rows(b), rest:] = mm(inv, u_ref[rows(b), rest:])
            for i in range(b + 1, nb):
                u_ref[rows(i), i * BLK :] -= mm_tn(
                    u_ref[rows(b), i * BLK : (i + 1) * BLK], u_ref[rows(b), i * BLK :]
                )

    last = inv_ref[rows(lb), :]
    wt_ref[rows(lb), :] = last.T
    right = -mm(u_ref[:lead, lead:], last.T)
    for b in range(lb - 1, -1, -1):
        part = right[b * BLK : (b + 1) * BLK, :]
        if b + 1 < lb:
            part = part - mm(u_ref[rows(b), (b + 1) * BLK : lead], wt_ref[(b + 1) * BLK : lead, :])
        wt_ref[rows(b), :] = mm_tn(inv_ref[rows(b), :], part)

    wt = halves(wt_ref[...])

    def slopes(r, carry):
        here = pl.ds(pl.multiple_of(r * BLK, BLK), BLK)
        for k in range(4):
            diff = xc[here, k : k + 1] - xr[k : k + 1, :]
            h_ref[here, k * BLK : (k + 1) * BLK] = split_dot(
                halves(c_ref[here, :] * (diff * diff)), wt, ((1,), (0,))
            )
        h_ref[here, 4 * BLK :] = nugget * wt_ref[here, :]
        return carry

    lax.fori_loop(0, nb, slopes, 0)
    z_ref[...] = split_dot(wt, halves(h_ref[...]), ((0,), (0,)))
    forward(u_ref, inv_ref, h_ref, lb)

    def h_of(i):
        i = 4 if i in (0, 5) else i - 1
        return h_ref[:lead, i * BLK : (i + 1) * BLK]

    def z_of(i):
        if i == 0:
            return eye - z_ref[:, 4 * BLK :]
        return z_ref[:, (i - 1) * BLK : i * BLK]

    lane1 = lax.broadcasted_iota(jnp.int32, (1, BLK), 1)
    out = jnp.zeros((1, BLK), F32)
    spot = 0
    for i in range(6):
        for j in range(i, 6):
            sign = -2.0 if (i == 0) != (j == 0) else 2.0
            both = sign * jnp.sum(h_of(i) * h_of(j), axis=0, keepdims=True)
            both = both + jnp.sum(z_of(i) * z_of(j), axis=0, keepdims=True)
            value = (0.5 * reps) * jnp.sum(both, axis=1, keepdims=True)
            out = out + jnp.where(lane1 == spot, value, 0.0)
            spot += 1


    left_here(ccrows.at[pl.ds(0, count - 1)], 0)
    near_down.wait_send()
    near_across.wait_send()
    for each in late:
        each.wait()
    field_down.wait()
    field_across.wait()
    landed(allc.at[pl.ds(0, (count - 1) * per_tile)], 5)
    left_here(allc.at[pl.ds(0, (count - 1) * per_tile)], 5)

    hot_c = onehot(cbuf[...], count * per_tile)
    hot_u = onehot(fbuf[:, :half], BLK) * alive
    hot_l = onehot(fbuf[:, half:], BLK)
    white = mm3_tn(mm3(hot_c, wt_ref[:nc, :]), allc[...]).T
    white = white + mm3(upper[...], mm3(hot_u, wt_ref[nc : nc + half, :]))
    white = white + mm3(left[...], mm3(hot_l, wt_ref[nc + half : lead, :]))
    white = white + mm3(own[...], wt_ref[lead:, :])
    white_ref[...] = white
    m_ref[:nc, :] = mm3_tn(hot_c, mm3(allc[...], white))
    m_ref[nc : nc + half, :] = mm3_tn(hot_u, mm3_tn(upper[...], white))
    m_ref[nc + half :, :] = mm3_tn(hot_l, mm3_tn(left[...], white))
    forward(u_ref, inv_ref, m_ref, lead // BLK)
    gram = mm3_tn(white, white)
    weight = 0.5 * gram - (0.5 * reps) * eye
    for i in range(6):
        at = 4 if i in (0, 5) else i - 1
        lead_part = jnp.sum(m_ref[...] * h_ref[:lead, at * BLK : (at + 1) * BLK], axis=0, keepdims=True)
        z = z_ref[:, at * BLK : (at + 1) * BLK]
        if i == 0:
            z = eye - z
            lead_part = -lead_part
        both = lead_part + jnp.sum(weight * z, axis=0, keepdims=True)
        value = jnp.sum(both, axis=1, keepdims=True)
        out = out + jnp.where(lane1 == 21 + i, value, 0.0)

    term[...] = out
    terms[pl.ds(me, 1), :] = out
    push(term, terms.at[pl.ds(me, 1)], 6)
    landed(terms.at[pl.ds(0, count - 1)], 6)
    total = jnp.sum(terms[...], axis=0, keepdims=True)
    cell = {}
    spot = 0
    for i in range(6):
        for j in range(i, 6):
            cell[i, j] = total[:, spot : spot + 1]
            spot += 1
    right_side = [total[:, 21 + i : 22 + i] for i in range(6)]
    for k in range(6):
        inv = 1.0 / cell[k, k]
        for i in range(k + 1, 6):
            ratio = cell[k, i] * inv
            for j in range(i, 6):
                cell[i, j] = cell[i, j] - ratio * cell[k, j]
            right_side[i] = right_side[i] - ratio * right_side[k]
    for k in range(5, -1, -1):
        acc = right_side[k]
        for j in range(k + 1, 6):
            acc = acc - cell[k, j] * right_side[j]
        right_side[k] = acc / cell[k, k]
    result = jnp.zeros((1, BLK), F32)
    for i in range(6):
        result = jnp.where(lane1 == i, right_side[i], result)
    step_ref[...] = result
    left_here(terms.at[pl.ds(0, count - 1)], 6)


def shape(*dims):
    return jax.ShapeDtypeStruct(dims, F32)


def body(coords, values, coarse_coords, coarse_values, fine_index, coarse_index, log_params):
    half = fine_index.shape[1] // 2
    reps, block = values.shape
    nc = coarse_index.shape[1]
    per_tile = coarse_coords.shape[1]
    n = nc + 2 * half + block
    lead = n - block
    count = lax.axis_size("row") * lax.axis_size("col")
    anywhere = pl.BlockSpec(memory_space=pl.ANY)
    inner = pl.BlockSpec(memory_space=pltpu.VMEM)
    step, white = pl.pallas_call(
        functools.partial(fused_kernel, per_tile),
        out_shape=[shape(1, BLK), shape(reps, block)],
        in_specs=[pl.BlockSpec(memory_space=pltpu.SMEM)] + [anywhere] * 6,
        out_specs=[inner, inner],
        scratch_shapes=[
            pltpu.VMEM((n, n), F32), pltpu.VMEM((n, BLK), F32), pltpu.VMEM((n, BLK), F32),
            pltpu.VMEM((n, 5 * BLK), F32), pltpu.VMEM((BLK, 5 * BLK), F32),
            pltpu.VMEM((n, n), F32), pltpu.VMEM((BLK, 2 * BLK), F32),
            pltpu.VMEM((8, n), F32), pltpu.VMEM((n, 8), F32), pltpu.VMEM((lead, BLK), F32),
            pltpu.VMEM((8, BLK), F32), pltpu.VMEM((2, 8, BLK), F32), pltpu.VMEM((4, per_tile), F32),
            pltpu.VMEM((1, BLK), F32), pltpu.VMEM((count, BLK), F32),
            pltpu.VMEM((1, nc), jnp.int32), pltpu.VMEM((1, 2 * half), jnp.int32),
            pltpu.VMEM((reps, block), F32), pltpu.VMEM((reps, block), F32),
            pltpu.VMEM((reps, block), F32), pltpu.VMEM((count * per_tile, reps), F32),
            pltpu.VMEM((1, BLK), F32), pltpu.VMEM((count, BLK), F32),
            pltpu.SemaphoreType.DMA((6,)), pltpu.SemaphoreType.DMA((7,)),
            pltpu.SemaphoreType.DMA((7,)),
        ],
        compiler_params=pltpu.CompilerParams(
            collective_id=0, has_side_effects=True, vmem_limit_bytes=56 * 1024 * 1024
        ),
    )(log_params, coords, coarse_coords, coarse_index, fine_index, values, coarse_values.T)
    return step[0, :6], white


def solution(mesh):
    in_specs = (
        P(None, ("row", "col")),
        P(None, ("row", "col")),
        P(None, ("row", "col")),
        P(None, ("row", "col")),
        P(("row", "col"), None),
        P(("row", "col"), None),
        P(),
    )
    out_specs = (P(), P(None, ("row", "col")))
    return jax.shard_map(body, mesh=mesh, in_specs=in_specs, out_specs=out_specs, check_vma=False)
```

```python
import functools
import math

import jax
import jax.numpy as jnp
from jax import lax
from jax.experimental import pallas as pl
from jax.experimental.pallas import tpu as pltpu
from jax.sharding import PartitionSpec as P

HIGH = lax.Precision.HIGHEST
ROOT_FIVE = math.sqrt(5.0)
NUGGET = 0.2
RANGE_BASE = (0.5, 0.5, 0.5, 0.5)
BLK = 128
PAN = 16
F32 = jnp.float32


def mm(a, b):
    return jnp.dot(a, b, precision=HIGH, preferred_element_type=F32)


def mm_tn(a, b):
    return lax.dot_general(
        a, b, (((0,), (0,)), ((), ())), precision=HIGH, preferred_element_type=F32
    )


def halves(x):
    high = x.astype(jnp.bfloat16)
    return high, (x - high.astype(F32)).astype(jnp.bfloat16)


def split_dot(a, b, dims):
    def dot(x, y):
        return lax.dot_general(x, y, (dims, ((), ())), preferred_element_type=F32)

    (ah, al), (bh, bl) = a, b
    return dot(ah, bh) + (dot(ah, bl) + dot(al, bh))


def mm3(a, b):
    return split_dot(halves(a), halves(b), ((1,), (0,)))


def mm3_tn(a, b):
    return split_dot(halves(a), halves(b), ((0,), (0,)))


def rows(b):
    return pl.ds(b * BLK, BLK)


def thirds(x):
    first = x.astype(jnp.bfloat16)
    rest = x - first.astype(F32)
    second = rest.astype(jnp.bfloat16)
    return first, second, (rest - second.astype(F32)).astype(jnp.bfloat16)


def outer_tn(x):
    a, b, c = thirds(x)
    left = jnp.concatenate([a, a, b, b, a, c], axis=0)[:, :BLK]
    right = jnp.concatenate([a, b, a, b, c, a], axis=0)
    return lax.dot_general(
        left, right, (((0,), (0,)), ((), ())), preferred_element_type=F32
    )


def spread_row(x, i):
    return jnp.broadcast_to(x[i : i + 1, :], (8, BLK))


def inverse_factor(s_ref):
    row8 = lax.broadcasted_iota(jnp.int32, (8, BLK), 0)
    panels = BLK // PAN
    own = PAN // 8
    va = [s_ref[g * 8 : g * 8 + 8, :BLK] for g in range(own)]
    vb = [s_ref[g * 8 : g * 8 + 8, BLK:] for g in range(own)]
    for p in range(panels):
        base = p * PAN
        groups = 2 * own if p + 1 < panels else own
        for g in range(own, groups):
            at = base + g * 8
            va.append(s_ref[at : at + 8, :BLK])
            vb.append(s_ref[at : at + 8, BLK:])
        cols = [
            [
                jnp.broadcast_to(va[g][:, base + j : base + j + 1], (8, BLK)) if g >= j // 8 else None
                for g in range(groups)
            ]
            for j in range(PAN)
        ]
        pivots = [jnp.ones((8, BLK), F32)] * own
        for k in range(PAN):
            gk, kk = divmod(k, 8)
            pivot = spread_row(cols[k][gk], kk)
            pivots[gk] = jnp.where(row8 == kk, pivot, pivots[gk])
            inv = 1.0 / pivot
            low = [cols[k][g] * inv if g >= gk else None for g in range(groups)]
            low[gk] = jnp.where(row8 > kk, low[gk], 0.0)
            for j in range(k + 1, PAN):
                other = spread_row(cols[k][j // 8], j % 8)
                for g in range(j // 8, groups):
                    cols[j][g] = cols[j][g] - low[g] * other
            xa, xb = spread_row(va[gk], kk), spread_row(vb[gk], kk)
            for g in range(gk, groups):
                va[g] = va[g] - low[g] * xa
                vb[g] = vb[g] - low[g] * xb
        for g in range(own):
            unit = lax.rsqrt(pivots[g])
            va[g] = va[g] * unit
            vb[g] = vb[g] * unit
            s_ref[base + g * 8 : base + g * 8 + 8, BLK:] = vb[g]
        done = base + 2 * PAN
        if done < BLK:
            top = jnp.concatenate(
                [jnp.concatenate(va[:own], axis=0), jnp.concatenate(vb[:own], axis=0)], axis=1
            )
            s_ref[done:, :] -= outer_tn(top)[done:, :]
        va, vb = va[own:], vb[own:]


def dot(a, b, dims=((1,), (0,))):
    return lax.dot_general(a, b, (dims, ((), ())), preferred_element_type=F32)


def beside(pair):
    return jnp.concatenate(pair, axis=1)


def folded(x):
    half = x.shape[1] // 2
    return x[:, :half] + x[:, half:]


def mm3_wide(a, b):
    (ah, al), (bh, bl) = a, b
    return folded(dot(ah, beside((bh, bl)))) + dot(al, bh)


MESH = pl.DeviceIdType.MESH


def onehot(index, count):
    return (lax.broadcasted_iota(jnp.int32, (count, index.shape[1]), 0) == index).astype(F32)


def onehot_rows(index, count):
    column = jnp.broadcast_to(index, (8, index.shape[1])).T[:, :1]
    return (lax.broadcasted_iota(jnp.int32, (index.shape[1], count), 1) == column).astype(F32)


def fused_kernel(
    per_tile, params, coords, ccoords, cidx, fidx, values, coarse, step_ref, white_ref,
    u_ref, li_ref, lt_ref, wt_ref, h_ref, z_ref, c_ref, s_ref, xr, xc, m_ref, pay, near, ccv, ccrow, ccrows,
    lp, cbuf, fbuf, hot_ref, pick_ref, own, upper, left, allc, term, terms, local_sem, send_sem, recv_sem,
):
    n_row, n_col = lax.axis_size("row"), lax.axis_size("col")
    count = n_row * n_col
    row, col = lax.axis_index("row"), lax.axis_index("col")
    me = row * n_col + col
    reps = values.shape[0]
    n = xr.shape[1]
    nb = n // BLK
    lead = n - BLK
    lb = nb - 1
    nc = cidx.shape[1]
    half = fidx.shape[1] // 2

    def place(d):
        other = lax.rem(me + d, count)
        return {"row": other // n_col, "col": lax.rem(other, n_col)}

    barrier = pltpu.get_barrier_semaphore()

    def greet(d, carry):
        pl.semaphore_signal(barrier, inc=1, device_id=place(d), device_id_type=MESH)
        return carry

    def fetch(src, dst, k):
        return pltpu.make_async_copy(src, dst, local_sem.at[k])

    early = [
        fetch(coords, pay.at[pl.ds(0, 4)], 0), fetch(ccoords, ccv, 1),
        fetch(cidx, cbuf, 2), fetch(fidx, fbuf, 3), fetch(params, lp, 6),
    ]
    late = [
        fetch(values, own, 4), fetch(coarse, allc.at[pl.ds(me * per_tile, per_tile)], 5),
    ]
    for each in early:
        each.start()
    lax.fori_loop(1, count, greet, 0)
    pay[4:, :] = jnp.zeros((4, BLK), F32)
    early[0].wait()
    early[1].wait()
    small = ccv[...]
    line = jnp.zeros((1, BLK), F32)
    wide = jnp.concatenate([small, jnp.zeros((4, BLK - per_tile), F32)], axis=1)
    for k in range(4):
        part = wide[k : k + 1, :]
        line = line + (pltpu.roll(part, k * per_tile, 1) if k else part)
    ccrow[...] = line
    ccrows[pl.ds(me, 1), :] = line
    pl.semaphore_wait(barrier, count - 1)

    def send(src, dst, k, where):
        return pltpu.make_async_remote_copy(
            src_ref=src, dst_ref=dst, send_sem=send_sem.at[k], recv_sem=recv_sem.at[k],
            device_id=where, device_id_type=MESH,
        )

    def push(src, dst, k):
        for dc in sorted(range(n_col), key=lambda d: -min(d, n_col - d)):

            def step(dr, carry, dc=dc):
                there = {"row": lax.rem(row + dr, n_row), "col": lax.rem(col + dc, n_col)}
                send(src, dst, k, there).start()
                return carry

            lax.fori_loop(0 if dc else 1, n_row, step, 0)

    def landed(ref, k):
        pltpu.make_async_copy(ref, ref, recv_sem.at[k]).wait()

    def left_here(ref, k):
        pltpu.make_async_copy(ref, ref, send_sem.at[k]).wait()

    down = {"row": lax.rem(row + 1, n_row)}
    across = {"col": lax.rem(col + 1, n_col)}
    push(ccrow, ccrows.at[pl.ds(me, 1)], 0)
    near_down = send(pay, near.at[0], 1, down)
    near_across = send(pay, near.at[1], 2, across)
    near_down.start()
    near_across.start()
    for each in late:
        each.start()
    field_down = send(values, upper, 3, down)
    field_across = send(values, left, 4, across)
    field_down.start()
    field_across.start()
    mine = allc.at[pl.ds(me * per_tile, per_tile)]
    for dc in sorted(range(1, n_col), key=lambda d: -min(d, n_col - d)):
        send(coarse, mine, 5, {"col": lax.rem(col + dc, n_col)}).start()

    early[4].wait()
    row8 = lax.broadcasted_iota(jnp.int32, (8, BLK), 0)
    spread = jnp.zeros((8, BLK), F32)
    for k in range(4):
        spread = jnp.where(row8 == k, lp[1 + k], spread)
    base = jnp.ones((8, BLK), F32)
    for k in range(4):
        base = jnp.where(row8 == k, RANGE_BASE[k], base)
    scale = (1.0 / (jnp.exp(spread) * base))[:, :1]
    variance = jnp.exp(jnp.full((1, BLK), lp[0], F32))[:, :1]
    nugget = (NUGGET * jnp.exp(jnp.full((1, BLK), lp[5], F32)))[:, :1]
    alive = jnp.where(row > 0, 1.0, 0.0)

    early[2].wait()
    early[3].wait()
    wanted = cbuf[...]
    tile = wanted // per_tile
    slot = wanted - tile * per_tile
    hot_t = onehot(tile, count)
    hot_s = onehot(slot, per_tile)
    pick_u = onehot(fbuf[:, :half], BLK)
    pick_l = onehot(fbuf[:, half:], BLK)
    hot_ref[...] = onehot_rows(wanted, count * per_tile).astype(jnp.bfloat16)
    pick_ref[:half, :] = (onehot_rows(fbuf[:, :half], BLK) * alive).astype(jnp.bfloat16)
    pick_ref[half:, :] = onehot_rows(fbuf[:, half:], BLK).astype(jnp.bfloat16)

    near_down.wait_recv()
    near_across.wait_recv()
    xr[:, nc : nc + half] = mm(near[0], pick_u) * (scale * alive)
    xr[:, nc + half : lead] = mm(near[1], pick_l) * scale
    xr[:, lead:] = pay[...] * scale
    landed(ccrows.at[pl.ds(0, count - 1)], 0)
    lines = mm_tn(ccrows[...], hot_t)
    for k in range(4):
        part = lines[k * per_tile : (k + 1) * per_tile, :] * hot_s
        xr[k : k + 1, :nc] = jnp.sum(part, axis=0, keepdims=True) * scale[k : k + 1, :]
    xr[5:, :nc] = jnp.zeros((3, nc), F32)
    point = lax.broadcasted_iota(jnp.int32, (1, n), 1)
    xr[4:5, :] = jnp.where((point >= nc) & (point < nc + half), alive, 1.0)
    for b in range(nb):
        xc[rows(b), :] = xr[:, b * BLK : (b + 1) * BLK].T

    def cover(r, carry):
        start = pl.multiple_of(r * 64, 64)
        here = pl.ds(start, 64)
        total = None
        for k in range(4):
            diff = xc[here, k : k + 1] - xr[k : k + 1, :]
            total = diff * diff if total is None else total + diff * diff
        live_c = xc[here, 4:5]
        paired = live_c * xr[4:5, :]
        root = ROOT_FIVE * jnp.sqrt(total)
        decay = jnp.exp(-root) * (variance * paired)
        ident = (
            lax.broadcasted_iota(jnp.int32, (64, n), 0) + start
            == lax.broadcasted_iota(jnp.int32, (64, n), 1)
        )
        u_ref[here, :] = (1.0 + root + root * root / 3.0) * decay + jnp.where(
            ident, live_c * nugget + 1.0 - live_c, 0.0
        )
        c_ref[here, :] = (5.0 / 3.0) * (1.0 + root) * decay
        return carry

    lax.fori_loop(0, n // 64, cover, 0)

    eye = (
        lax.broadcasted_iota(jnp.int32, (BLK, BLK), 0)
        == lax.broadcasted_iota(jnp.int32, (BLK, BLK), 1)
    ).astype(F32)
    for b in range(nb):
        s_ref[:, :BLK] = u_ref[rows(b), b * BLK : (b + 1) * BLK]
        s_ref[:, BLK:] = eye
        inverse_factor(s_ref)
        inv = s_ref[:, BLK:]
        if b == 0:
            late[1].wait()
            landed(allc.at[pl.ds(0, (n_col - 1) * per_tile)], 5)
            band = allc.at[pl.ds(row * (n_col * per_tile), n_col * per_tile)]
            for dr in range(1, n_row):
                send(band, band, 7, {"row": lax.rem(row + dr, n_row)}).start()
        if b == lb:
            break
        here, rest = b * BLK, (b + 1) * BLK
        u_ref[rows(b), rest:] = mm(inv, u_ref[rows(b), rest:])
        for i in range(b + 1, nb):
            u_ref[rows(i), i * BLK :] -= mm_tn(
                u_ref[rows(b), i * BLK : (i + 1) * BLK], u_ref[rows(b), i * BLK :]
            )
        li_ref[rows(b), here:rest] = inv
        lt_ref[rows(b), here:rest] = inv.T
        if b:
            above = mm_tn(u_ref[:here, here:rest], li_ref[:here, :here])
            side = -mm(inv, above)
            li_ref[rows(b), :here] = side
            for i in range(b):
                lt_ref[rows(i), here:rest] = side[:, i * BLK : (i + 1) * BLK].T
                li_ref[rows(i), here:rest] = jnp.zeros((BLK, BLK), F32)
                lt_ref[rows(b), i * BLK : (i + 1) * BLK] = jnp.zeros((BLK, BLK), F32)

    turned = inv.T
    wt_ref[lead:, :] = turned
    wt_ref[:lead, :] = -mm(lt_ref[...], mm(u_ref[:lead, lead:], turned))

    wt = halves(wt_ref[...])
    wide = beside(wt)

    def slopes(r, carry):
        here = pl.ds(pl.multiple_of(r * BLK, BLK), BLK)
        for k in range(4):
            diff = xc[here, k : k + 1] - xr[k : k + 1, :]
            high, low = halves(c_ref[here, :] * (diff * diff))
            h_ref[here, k * BLK : (k + 1) * BLK] = folded(dot(high, wide)) + dot(low, wt[0])
        h_ref[here, 4 * BLK :] = nugget * wt_ref[here, :]
        return carry

    lax.fori_loop(0, nb, slopes, 0)
    z_ref[...] = split_dot(wt, halves(h_ref[...]), ((0,), (0,)))
    lower = halves(li_ref[...])
    h_ref[:lead, :] = split_dot(lower, halves(h_ref[:lead, :]), ((1,), (0,)))

    def h_of(i):
        i = 4 if i in (0, 5) else i - 1
        return h_ref[:lead, i * BLK : (i + 1) * BLK]

    def z_of(i):
        if i == 0:
            return eye - z_ref[:, 4 * BLK :]
        return z_ref[:, (i - 1) * BLK : i * BLK]

    lane1 = lax.broadcasted_iota(jnp.int32, (1, BLK), 1)
    out = jnp.zeros((1, BLK), F32)
    spot = 0
    for i in range(6):
        for j in range(i, 6):
            sign = -2.0 if (i == 0) != (j == 0) else 2.0
            both = sign * jnp.sum(h_of(i) * h_of(j), axis=0, keepdims=True)
            both = both + jnp.sum(z_of(i) * z_of(j), axis=0, keepdims=True)
            value = (0.5 * reps) * jnp.sum(both, axis=1, keepdims=True)
            out = out + jnp.where(lane1 == spot, value, 0.0)
            spot += 1


    left_here(ccrows.at[pl.ds(0, count - 1)], 0)
    near_down.wait_send()
    near_across.wait_send()
    late[0].wait()
    field_down.wait()
    field_across.wait()
    left_here(allc.at[pl.ds(0, (n_col - 1) * per_tile)], 5)
    landed(allc.at[pl.ds(0, (n_row - 1) * n_col * per_tile)], 7)
    left_here(allc.at[pl.ds(0, (n_row - 1) * n_col * per_tile)], 7)

    hot_c = hot_ref[...]
    pick = pick_ref[...]
    coarse_wide = dot(hot_c, wide[:nc, :], ((0,), (0,))).astype(jnp.bfloat16)
    high, low = halves(allc[...])
    both = dot(coarse_wide, high, ((0,), (0,)))
    white = (both[:BLK, :] + both[BLK:, :] + dot(coarse_wide[:, :BLK], low, ((0,), (0,)))).T
    near_wide = jnp.concatenate(
        [
            dot(pick[:half, :], wide[nc : nc + half, :], ((0,), (0,))).astype(jnp.bfloat16),
            dot(pick[half:, :], wide[nc + half : lead, :], ((0,), (0,))).astype(jnp.bfloat16),
            wide[lead:, :],
        ],
        axis=0,
    )
    fields = halves(jnp.concatenate([upper[...], left[...], own[...]], axis=1))
    white = white + folded(dot(fields[0], near_wide)) + dot(fields[1], near_wide[:, :BLK])
    white_ref[...] = white
    parts = halves(white)
    white_wide = beside(parts)
    seen = folded(dot(high, white_wide)) + dot(low, parts[0])
    m_ref[:nc, :] = folded(dot(hot_c, beside(halves(seen))))
    seen = folded(dot(fields[0][:, : 2 * BLK], white_wide, ((0,), (0,)))) + dot(
        fields[1][:, : 2 * BLK], parts[0], ((0,), (0,))
    )
    seen = beside(halves(seen))
    m_ref[nc : nc + half, :] = folded(dot(pick[:half, :], seen[:BLK, :]))
    m_ref[nc + half :, :] = folded(dot(pick[half:, :], seen[BLK:, :]))
    m_ref[...] = mm3_wide(lower, halves(m_ref[...]))
    gram = mm3_tn(white, white)
    weight = 0.5 * gram - (0.5 * reps) * eye
    for i in range(6):
        at = 4 if i in (0, 5) else i - 1
        lead_part = jnp.sum(m_ref[...] * h_ref[:lead, at * BLK : (at + 1) * BLK], axis=0, keepdims=True)
        z = z_ref[:, at * BLK : (at + 1) * BLK]
        if i == 0:
            z = eye - z
            lead_part = -lead_part
        both = lead_part + jnp.sum(weight * z, axis=0, keepdims=True)
        value = jnp.sum(both, axis=1, keepdims=True)
        out = out + jnp.where(lane1 == 21 + i, value, 0.0)

    term[...] = out
    terms[pl.ds(me, 1), :] = out
    push(term, terms.at[pl.ds(me, 1)], 6)
    landed(terms.at[pl.ds(0, count - 1)], 6)
    total = jnp.sum(terms[...], axis=0, keepdims=True)
    cell = {}
    spot = 0
    for i in range(6):
        for j in range(i, 6):
            cell[i, j] = total[:, spot : spot + 1]
            spot += 1
    right_side = [total[:, 21 + i : 22 + i] for i in range(6)]
    for k in range(6):
        inv = 1.0 / cell[k, k]
        for i in range(k + 1, 6):
            ratio = cell[k, i] * inv
            for j in range(i, 6):
                cell[i, j] = cell[i, j] - ratio * cell[k, j]
            right_side[i] = right_side[i] - ratio * right_side[k]
    for k in range(5, -1, -1):
        acc = right_side[k]
        for j in range(k + 1, 6):
            acc = acc - cell[k, j] * right_side[j]
        right_side[k] = acc / cell[k, k]
    result = jnp.zeros((1, BLK), F32)
    for i in range(6):
        result = jnp.where(lane1 == i, right_side[i], result)
    step_ref[...] = result[:, :6]
    left_here(terms.at[pl.ds(0, count - 1)], 6)


def shape(*dims):
    return jax.ShapeDtypeStruct(dims, F32)


def body(coords, values, coarse_coords, coarse_values, fine_index, coarse_index, log_params):
    half = fine_index.shape[1] // 2
    reps, block = values.shape
    nc = coarse_index.shape[1]
    per_tile = coarse_coords.shape[1]
    n = nc + 2 * half + block
    lead = n - block
    count = lax.axis_size("row") * lax.axis_size("col")
    anywhere = pl.BlockSpec(memory_space=pl.ANY)
    inner = pl.BlockSpec(memory_space=pltpu.VMEM)
    arguments = (
        log_params, coords, coarse_coords, coarse_index, fine_index, values, coarse_values.T
    )
    step, white = pl.pallas_call(
        functools.partial(fused_kernel, per_tile),
        out_shape=[shape(1, 6), shape(reps, block)],
        in_specs=[anywhere] * len(arguments),
        out_specs=[inner, inner],
        scratch_shapes=[
            pltpu.VMEM((n, n), F32), pltpu.VMEM((lead, lead), F32), pltpu.VMEM((lead, lead), F32),
            pltpu.VMEM((n, BLK), F32),
            pltpu.VMEM((n, 5 * BLK), F32), pltpu.VMEM((BLK, 5 * BLK), F32),
            pltpu.VMEM((n, n), F32), pltpu.VMEM((BLK, 2 * BLK), F32),
            pltpu.VMEM((8, n), F32), pltpu.VMEM((n, 8), F32), pltpu.VMEM((lead, BLK), F32),
            pltpu.VMEM((8, BLK), F32), pltpu.VMEM((2, 8, BLK), F32), pltpu.VMEM((4, per_tile), F32),
            pltpu.VMEM((1, BLK), F32), pltpu.VMEM((count, BLK), F32),
            pltpu.SMEM((6,), F32), pltpu.VMEM((1, nc), jnp.int32), pltpu.VMEM((1, 2 * half), jnp.int32),
            pltpu.VMEM((nc, count * per_tile), jnp.bfloat16),
            pltpu.VMEM((2 * half, BLK), jnp.bfloat16),
            pltpu.VMEM((reps, block), F32), pltpu.VMEM((reps, block), F32),
            pltpu.VMEM((reps, block), F32), pltpu.VMEM((count * per_tile, reps), F32),
            pltpu.VMEM((1, BLK), F32), pltpu.VMEM((count, BLK), F32),
            pltpu.SemaphoreType.DMA((7,)), pltpu.SemaphoreType.DMA((8,)),
            pltpu.SemaphoreType.DMA((8,)),
        ],
        compiler_params=pltpu.CompilerParams(
            collective_id=0, has_side_effects=True, vmem_limit_bytes=40 * 1024 * 1024
        ),
    )(*(pltpu.with_memory_space_constraint(x, pltpu.HBM) for x in arguments))
    return step[0], white


def solution(mesh):
    in_specs = (
        P(None, ("row", "col")),
        P(None, ("row", "col")),
        P(None, ("row", "col")),
        P(None, ("row", "col")),
        P(("row", "col"), None),
        P(("row", "col"), None),
        P(),
    )
    out_specs = (P(), P(None, ("row", "col")))
    return jax.shard_map(body, mesh=mesh, in_specs=in_specs, out_specs=out_specs, check_vma=False)
```

```python
import functools
import math

import jax
import jax.numpy as jnp
from jax import lax
from jax.experimental import pallas as pl
from jax.experimental.pallas import tpu as pltpu
from jax.sharding import PartitionSpec as P

HIGH = lax.Precision.HIGHEST
ROOT_FIVE = math.sqrt(5.0)
NUGGET = 0.2
RANGE_BASE = (0.5, 0.5, 0.5, 0.5)
BLK = 128
PAN = 16
F32 = jnp.float32


def mm(a, b):
    return jnp.dot(a, b, precision=HIGH, preferred_element_type=F32)


def mm_tn(a, b):
    return lax.dot_general(
        a, b, (((0,), (0,)), ((), ())), precision=HIGH, preferred_element_type=F32
    )


def halves(x):
    high = x.astype(jnp.bfloat16)
    return high, (x - high.astype(F32)).astype(jnp.bfloat16)


def split_dot(a, b, dims):
    def dot(x, y):
        return lax.dot_general(x, y, (dims, ((), ())), preferred_element_type=F32)

    (ah, al), (bh, bl) = a, b
    return dot(ah, bh) + (dot(ah, bl) + dot(al, bh))


def mm3(a, b):
    return split_dot(halves(a), halves(b), ((1,), (0,)))


def mm3_tn(a, b):
    return split_dot(halves(a), halves(b), ((0,), (0,)))


def rows(b):
    return pl.ds(b * BLK, BLK)


def thirds(x):
    first = x.astype(jnp.bfloat16)
    rest = x - first.astype(F32)
    second = rest.astype(jnp.bfloat16)
    return first, second, (rest - second.astype(F32)).astype(jnp.bfloat16)


def outer_tn(x):
    a, b, c = thirds(x)
    left = jnp.concatenate([a, a, b, b, a, c], axis=0)[:, :BLK]
    right = jnp.concatenate([a, b, a, b, c, a], axis=0)
    return lax.dot_general(
        left, right, (((0,), (0,)), ((), ())), preferred_element_type=F32
    )


def spread_row(x, i):
    return jnp.broadcast_to(x[i : i + 1, :], (8, BLK))


def inverse_factor(s_ref):
    row8 = lax.broadcasted_iota(jnp.int32, (8, BLK), 0)
    panels = BLK // PAN
    own = PAN // 8
    va = [s_ref[g * 8 : g * 8 + 8, :BLK] for g in range(own)]
    vb = [s_ref[g * 8 : g * 8 + 8, BLK:] for g in range(own)]
    for p in range(panels):
        base = p * PAN
        groups = 2 * own if p + 1 < panels else own
        for g in range(own, groups):
            at = base + g * 8
            va.append(s_ref[at : at + 8, :BLK])
            vb.append(s_ref[at : at + 8, BLK:])
        cols = [
            [
                jnp.broadcast_to(va[g][:, base + j : base + j + 1], (8, BLK)) if g >= j // 8 else None
                for g in range(groups)
            ]
            for j in range(PAN)
        ]
        pivots = [jnp.ones((8, BLK), F32)] * own
        for k in range(PAN):
            gk, kk = divmod(k, 8)
            pivot = spread_row(cols[k][gk], kk)
            pivots[gk] = jnp.where(row8 == kk, pivot, pivots[gk])
            inv = 1.0 / pivot
            low = [cols[k][g] * inv if g >= gk else None for g in range(groups)]
            low[gk] = jnp.where(row8 > kk, low[gk], 0.0)
            for j in range(k + 1, PAN):
                other = spread_row(cols[k][j // 8], j % 8)
                for g in range(j // 8, groups):
                    cols[j][g] = cols[j][g] - low[g] * other
            xa, xb = spread_row(va[gk], kk), spread_row(vb[gk], kk)
            for g in range(gk, groups):
                va[g] = va[g] - low[g] * xa
                vb[g] = vb[g] - low[g] * xb
        for g in range(own):
            unit = lax.rsqrt(pivots[g])
            va[g] = va[g] * unit
            vb[g] = vb[g] * unit
            s_ref[base + g * 8 : base + g * 8 + 8, BLK:] = vb[g]
        done = base + 2 * PAN
        if done < BLK:
            top = jnp.concatenate(
                [jnp.concatenate(va[:own], axis=0), jnp.concatenate(vb[:own], axis=0)], axis=1
            )
            s_ref[done:, :] -= outer_tn(top)[done:, :]
        va, vb = va[own:], vb[own:]


def dot(a, b, dims=((1,), (0,))):
    return lax.dot_general(a, b, (dims, ((), ())), preferred_element_type=F32)


def beside(pair):
    return jnp.concatenate(pair, axis=1)


def folded(x):
    half = x.shape[1] // 2
    return x[:, :half] + x[:, half:]


def mm3_wide(a, b):
    (ah, al), (bh, bl) = a, b
    return folded(dot(ah, beside((bh, bl)))) + dot(al, bh)


MESH = pl.DeviceIdType.MESH


def onehot(index, count):
    return (lax.broadcasted_iota(jnp.int32, (count, index.shape[1]), 0) == index).astype(F32)


def onehot_rows(index, count):
    column = jnp.broadcast_to(index, (8, index.shape[1])).T[:, :1]
    return (lax.broadcasted_iota(jnp.int32, (index.shape[1], count), 1) == column).astype(F32)


def fused_kernel(
    per_tile, params, coords, ccoords, cidx, fidx, values, coarse, step_ref, white_ref,
    u_ref, li_ref, lt_ref, wt_ref, h_ref, z_ref, c_ref, s_ref, xr, xc, m_ref, pay, near, ccv, ccrow, ccrows,
    lp, cbuf, fbuf, hot_ref, pick_ref, own, upper, left, allc, term, terms, local_sem, send_sem, recv_sem,
):
    n_row, n_col = lax.axis_size("row"), lax.axis_size("col")
    count = n_row * n_col
    row, col = lax.axis_index("row"), lax.axis_index("col")
    me = row * n_col + col
    reps = values.shape[0]
    n = xr.shape[1]
    nb = n // BLK
    lead = n - BLK
    lb = nb - 1
    nc = cidx.shape[1]
    half = fidx.shape[1] // 2

    def place(d):
        other = lax.rem(me + d, count)
        return {"row": other // n_col, "col": lax.rem(other, n_col)}

    barrier = pltpu.get_barrier_semaphore()

    def greet(d, carry):
        pl.semaphore_signal(barrier, inc=1, device_id=place(d), device_id_type=MESH)
        return carry

    def fetch(src, dst, k):
        return pltpu.make_async_copy(src, dst, local_sem.at[k])

    early = [
        fetch(coords, pay.at[pl.ds(0, 4)], 0), fetch(ccoords, ccv, 1),
        fetch(cidx, cbuf, 2), fetch(fidx, fbuf, 3), fetch(params, lp, 6),
    ]
    late = [
        fetch(values, own, 4), fetch(coarse, allc.at[pl.ds(me * per_tile, per_tile)], 5),
    ]
    for each in early:
        each.start()
    lax.fori_loop(1, count, greet, 0)
    pay[4:, :] = jnp.zeros((4, BLK), F32)
    early[0].wait()
    early[1].wait()
    small = ccv[...]
    line = jnp.zeros((1, BLK), F32)
    wide = jnp.concatenate([small, jnp.zeros((4, BLK - per_tile), F32)], axis=1)
    for k in range(4):
        part = wide[k : k + 1, :]
        line = line + (pltpu.roll(part, k * per_tile, 1) if k else part)
    ccrow[...] = line
    ccrows[pl.ds(me, 1), :] = line
    pl.semaphore_wait(barrier, count - 1)

    def send(src, dst, k, where):
        return pltpu.make_async_remote_copy(
            src_ref=src, dst_ref=dst, send_sem=send_sem.at[k], recv_sem=recv_sem.at[k],
            device_id=where, device_id_type=MESH,
        )

    def push(src, dst, k):
        for dc in sorted(range(n_col), key=lambda d: -min(d, n_col - d)):

            def step(dr, carry, dc=dc):
                there = {"row": lax.rem(row + dr, n_row), "col": lax.rem(col + dc, n_col)}
                send(src, dst, k, there).start()
                return carry

            lax.fori_loop(0 if dc else 1, n_row, step, 0)

    def landed(ref, k):
        pltpu.make_async_copy(ref, ref, recv_sem.at[k]).wait()

    def left_here(ref, k):
        pltpu.make_async_copy(ref, ref, send_sem.at[k]).wait()

    down = {"row": lax.rem(row + 1, n_row)}
    across = {"col": lax.rem(col + 1, n_col)}
    push(ccrow, ccrows.at[pl.ds(me, 1)], 0)
    near_down = send(pay, near.at[0], 1, down)
    near_across = send(pay, near.at[1], 2, across)
    near_down.start()
    near_across.start()
    early[4].wait()
    row8 = lax.broadcasted_iota(jnp.int32, (8, BLK), 0)
    spread = jnp.zeros((8, BLK), F32)
    for k in range(4):
        spread = jnp.where(row8 == k, lp[1 + k], spread)
    base = jnp.ones((8, BLK), F32)
    for k in range(4):
        base = jnp.where(row8 == k, RANGE_BASE[k], base)
    scale = (1.0 / (jnp.exp(spread) * base))[:, :1]
    variance = jnp.exp(jnp.full((1, BLK), lp[0], F32))[:, :1]
    nugget = (NUGGET * jnp.exp(jnp.full((1, BLK), lp[5], F32)))[:, :1]
    alive = jnp.where(row > 0, 1.0, 0.0)

    early[2].wait()
    early[3].wait()
    wanted = cbuf[...]
    tile = wanted // per_tile
    slot = wanted - tile * per_tile
    hot_t = onehot(tile, count)
    hot_s = onehot(slot, per_tile)
    pick_u = onehot(fbuf[:, :half], BLK)
    pick_l = onehot(fbuf[:, half:], BLK)
    hot_ref[...] = onehot_rows(wanted, count * per_tile).astype(jnp.bfloat16)
    pick_ref[:half, :] = (onehot_rows(fbuf[:, :half], BLK) * alive).astype(jnp.bfloat16)
    pick_ref[half:, :] = onehot_rows(fbuf[:, half:], BLK).astype(jnp.bfloat16)

    near_down.wait_recv()
    near_across.wait_recv()
    xr[:, nc : nc + half] = mm(near[0], pick_u) * (scale * alive)
    xr[:, nc + half : lead] = mm(near[1], pick_l) * scale
    xr[:, lead:] = pay[...] * scale
    landed(ccrows.at[pl.ds(0, count - 1)], 0)
    for each in late:
        each.start()
    field_down = send(values, upper, 3, down)
    field_across = send(values, left, 4, across)
    mine = allc.at[pl.ds(me * per_tile, per_tile)]
    for dc in sorted(range(1, n_col), key=lambda d: -min(d, n_col - d)):
        send(coarse, mine, 5, {"col": lax.rem(col + dc, n_col)}).start()

    lines = mm_tn(ccrows[...], hot_t)
    for k in range(4):
        part = lines[k * per_tile : (k + 1) * per_tile, :] * hot_s
        xr[k : k + 1, :nc] = jnp.sum(part, axis=0, keepdims=True) * scale[k : k + 1, :]
    xr[5:, :nc] = jnp.zeros((3, nc), F32)
    point = lax.broadcasted_iota(jnp.int32, (1, n), 1)
    xr[4:5, :] = jnp.where((point >= nc) & (point < nc + half), alive, 1.0)
    for b in range(nb):
        xc[rows(b), :] = xr[:, b * BLK : (b + 1) * BLK].T

    def cover(r, carry):
        start = pl.multiple_of(r * 64, 64)
        here = pl.ds(start, 64)
        total = None
        for k in range(4):
            diff = xc[here, k : k + 1] - xr[k : k + 1, :]
            total = diff * diff if total is None else total + diff * diff
        live_c = xc[here, 4:5]
        paired = live_c * xr[4:5, :]
        root = ROOT_FIVE * jnp.sqrt(total)
        decay = jnp.exp(-root) * (variance * paired)
        ident = (
            lax.broadcasted_iota(jnp.int32, (64, n), 0) + start
            == lax.broadcasted_iota(jnp.int32, (64, n), 1)
        )
        u_ref[here, :] = (1.0 + root + root * root / 3.0) * decay + jnp.where(
            ident, live_c * nugget + 1.0 - live_c, 0.0
        )
        c_ref[here, :] = (5.0 / 3.0) * (1.0 + root) * decay
        return carry

    lax.fori_loop(0, n // 64, cover, 0)

    eye = (
        lax.broadcasted_iota(jnp.int32, (BLK, BLK), 0)
        == lax.broadcasted_iota(jnp.int32, (BLK, BLK), 1)
    ).astype(F32)
    def band(line):
        return allc.at[pl.ds(line * (n_col * per_tile), n_col * per_tile)]

    pair = n_row // 2
    sibling = {"row": row + 1 - 2 * lax.rem(row, 2)}
    for b in range(nb):
        s_ref[:, :BLK] = u_ref[rows(b), b * BLK : (b + 1) * BLK]
        s_ref[:, BLK:] = eye
        inverse_factor(s_ref)
        inv = s_ref[:, BLK:]
        if b == 1:
            late[1].wait()
            landed(allc.at[pl.ds(0, (n_col - 1) * per_tile)], 5)
            for k in range(1, pair):
                send(band(row), band(row), 7, {"row": lax.rem(row + 2 * k, n_row)}).start()
            field_down.start()
            field_across.start()
        if b == lb:
            break
        here, rest = b * BLK, (b + 1) * BLK
        u_ref[rows(b), rest:] = mm(inv, u_ref[rows(b), rest:])
        for i in range(b + 1, nb):
            u_ref[rows(i), i * BLK :] -= mm_tn(
                u_ref[rows(b), i * BLK : (i + 1) * BLK], u_ref[rows(b), i * BLK :]
            )
        li_ref[rows(b), here:rest] = inv
        lt_ref[rows(b), here:rest] = inv.T
        if b:
            above = mm_tn(u_ref[:here, here:rest], li_ref[:here, :here])
            side = -mm(inv, above)
            li_ref[rows(b), :here] = side
            for i in range(b):
                lt_ref[rows(i), here:rest] = side[:, i * BLK : (i + 1) * BLK].T
                li_ref[rows(i), here:rest] = jnp.zeros((BLK, BLK), F32)
                lt_ref[rows(b), i * BLK : (i + 1) * BLK] = jnp.zeros((BLK, BLK), F32)

    turned = inv.T
    wt_ref[lead:, :] = turned
    wt_ref[:lead, :] = -mm(lt_ref[...], mm(u_ref[:lead, lead:], turned))

    wt = halves(wt_ref[...])
    wide = beside(wt)

    def slopes(r, carry):
        here = pl.ds(pl.multiple_of(r * BLK, BLK), BLK)
        for k in range(4):
            diff = xc[here, k : k + 1] - xr[k : k + 1, :]
            high, low = halves(c_ref[here, :] * (diff * diff))
            h_ref[here, k * BLK : (k + 1) * BLK] = folded(dot(high, wide)) + dot(low, wt[0])
        h_ref[here, 4 * BLK :] = nugget * wt_ref[here, :]
        return carry

    lax.fori_loop(0, nb, slopes, 0)
    landed(allc.at[pl.ds(0, (pair - 1) * n_col * per_tile)], 7)
    for k in range(pair):
        line = lax.rem(row + 2 * k, n_row)
        send(band(line), band(line), 8, sibling).start()
    z_ref[...] = split_dot(wt, halves(h_ref[...]), ((0,), (0,)))
    lower = halves(li_ref[...])
    h_ref[:lead, :] = split_dot(lower, halves(h_ref[:lead, :]), ((1,), (0,)))

    def h_of(i):
        i = 4 if i in (0, 5) else i - 1
        return h_ref[:lead, i * BLK : (i + 1) * BLK]

    def z_of(i):
        if i == 0:
            return eye - z_ref[:, 4 * BLK :]
        return z_ref[:, (i - 1) * BLK : i * BLK]

    lane1 = lax.broadcasted_iota(jnp.int32, (1, BLK), 1)
    out = jnp.zeros((1, BLK), F32)
    spot = 0
    for i in range(6):
        for j in range(i, 6):
            sign = -2.0 if (i == 0) != (j == 0) else 2.0
            both = sign * jnp.sum(h_of(i) * h_of(j), axis=0, keepdims=True)
            both = both + jnp.sum(z_of(i) * z_of(j), axis=0, keepdims=True)
            value = (0.5 * reps) * jnp.sum(both, axis=1, keepdims=True)
            out = out + jnp.where(lane1 == spot, value, 0.0)
            spot += 1


    left_here(ccrows.at[pl.ds(0, count - 1)], 0)
    near_down.wait_send()
    near_across.wait_send()
    late[0].wait()
    field_down.wait()
    field_across.wait()
    left_here(allc.at[pl.ds(0, (n_col - 1) * per_tile)], 5)
    left_here(allc.at[pl.ds(0, (pair - 1) * n_col * per_tile)], 7)
    landed(allc.at[pl.ds(0, pair * n_col * per_tile)], 8)
    left_here(allc.at[pl.ds(0, pair * n_col * per_tile)], 8)

    hot_c = hot_ref[...]
    pick = pick_ref[...]
    coarse_wide = dot(hot_c, wide[:nc, :], ((0,), (0,))).astype(jnp.bfloat16)
    high, low = halves(allc[...])
    both = dot(coarse_wide, high, ((0,), (0,)))
    white = (both[:BLK, :] + both[BLK:, :] + dot(coarse_wide[:, :BLK], low, ((0,), (0,)))).T
    near_wide = jnp.concatenate(
        [
            dot(pick[:half, :], wide[nc : nc + half, :], ((0,), (0,))).astype(jnp.bfloat16),
            dot(pick[half:, :], wide[nc + half : lead, :], ((0,), (0,))).astype(jnp.bfloat16),
            wide[lead:, :],
        ],
        axis=0,
    )
    fields = halves(jnp.concatenate([upper[...], left[...], own[...]], axis=1))
    white = white + folded(dot(fields[0], near_wide)) + dot(fields[1], near_wide[:, :BLK])
    white_ref[...] = white
    parts = halves(white)
    white_wide = beside(parts)
    seen = folded(dot(high, white_wide)) + dot(low, parts[0])
    m_ref[:nc, :] = folded(dot(hot_c, beside(halves(seen))))
    seen = folded(dot(fields[0][:, : 2 * BLK], white_wide, ((0,), (0,)))) + dot(
        fields[1][:, : 2 * BLK], parts[0], ((0,), (0,))
    )
    seen = beside(halves(seen))
    m_ref[nc : nc + half, :] = folded(dot(pick[:half, :], seen[:BLK, :]))
    m_ref[nc + half :, :] = folded(dot(pick[half:, :], seen[BLK:, :]))
    m_ref[...] = mm3_wide(lower, halves(m_ref[...]))
    gram = mm3_tn(white, white)
    weight = 0.5 * gram - (0.5 * reps) * eye
    for i in range(6):
        at = 4 if i in (0, 5) else i - 1
        lead_part = jnp.sum(m_ref[...] * h_ref[:lead, at * BLK : (at + 1) * BLK], axis=0, keepdims=True)
        z = z_ref[:, at * BLK : (at + 1) * BLK]
        if i == 0:
            z = eye - z
            lead_part = -lead_part
        both = lead_part + jnp.sum(weight * z, axis=0, keepdims=True)
        value = jnp.sum(both, axis=1, keepdims=True)
        out = out + jnp.where(lane1 == 21 + i, value, 0.0)

    term[...] = out
    terms[pl.ds(me, 1), :] = out
    push(term, terms.at[pl.ds(me, 1)], 6)
    landed(terms.at[pl.ds(0, count - 1)], 6)
    total = jnp.sum(terms[...], axis=0, keepdims=True)
    cell = {}
    spot = 0
    for i in range(6):
        for j in range(i, 6):
            cell[i, j] = total[:, spot : spot + 1]
            spot += 1
    right_side = [total[:, 21 + i : 22 + i] for i in range(6)]
    for k in range(6):
        inv = 1.0 / cell[k, k]
        for i in range(k + 1, 6):
            ratio = cell[k, i] * inv
            for j in range(i, 6):
                cell[i, j] = cell[i, j] - ratio * cell[k, j]
            right_side[i] = right_side[i] - ratio * right_side[k]
    for k in range(5, -1, -1):
        acc = right_side[k]
        for j in range(k + 1, 6):
            acc = acc - cell[k, j] * right_side[j]
        right_side[k] = acc / cell[k, k]
    result = jnp.zeros((1, BLK), F32)
    for i in range(6):
        result = jnp.where(lane1 == i, right_side[i], result)
    step_ref[...] = result[:, :6]
    left_here(terms.at[pl.ds(0, count - 1)], 6)


def shape(*dims):
    return jax.ShapeDtypeStruct(dims, F32)


def body(coords, values, coarse_coords, coarse_values, fine_index, coarse_index, log_params):
    half = fine_index.shape[1] // 2
    reps, block = values.shape
    nc = coarse_index.shape[1]
    per_tile = coarse_coords.shape[1]
    n = nc + 2 * half + block
    lead = n - block
    count = lax.axis_size("row") * lax.axis_size("col")
    anywhere = pl.BlockSpec(memory_space=pl.ANY)
    inner = pl.BlockSpec(memory_space=pltpu.VMEM)
    arguments = (
        log_params, coords, coarse_coords, coarse_index, fine_index, values, coarse_values.T
    )
    step, white = pl.pallas_call(
        functools.partial(fused_kernel, per_tile),
        out_shape=[shape(1, 6), shape(reps, block)],
        in_specs=[anywhere] * len(arguments),
        out_specs=[inner, inner],
        scratch_shapes=[
            pltpu.VMEM((n, n), F32), pltpu.VMEM((lead, lead), F32), pltpu.VMEM((lead, lead), F32),
            pltpu.VMEM((n, BLK), F32),
            pltpu.VMEM((n, 5 * BLK), F32), pltpu.VMEM((BLK, 5 * BLK), F32),
            pltpu.VMEM((n, n), F32), pltpu.VMEM((BLK, 2 * BLK), F32),
            pltpu.VMEM((8, n), F32), pltpu.VMEM((n, 8), F32), pltpu.VMEM((lead, BLK), F32),
            pltpu.VMEM((8, BLK), F32), pltpu.VMEM((2, 8, BLK), F32), pltpu.VMEM((4, per_tile), F32),
            pltpu.VMEM((1, BLK), F32), pltpu.VMEM((count, BLK), F32),
            pltpu.SMEM((6,), F32), pltpu.VMEM((1, nc), jnp.int32), pltpu.VMEM((1, 2 * half), jnp.int32),
            pltpu.VMEM((nc, count * per_tile), jnp.bfloat16),
            pltpu.VMEM((2 * half, BLK), jnp.bfloat16),
            pltpu.VMEM((reps, block), F32), pltpu.VMEM((reps, block), F32),
            pltpu.VMEM((reps, block), F32), pltpu.VMEM((count * per_tile, reps), F32),
            pltpu.VMEM((1, BLK), F32), pltpu.VMEM((count, BLK), F32),
            pltpu.SemaphoreType.DMA((7,)), pltpu.SemaphoreType.DMA((9,)),
            pltpu.SemaphoreType.DMA((9,)),
        ],
        compiler_params=pltpu.CompilerParams(
            collective_id=0, has_side_effects=True, vmem_limit_bytes=40 * 1024 * 1024
        ),
    )(*(pltpu.with_memory_space_constraint(x, pltpu.HBM) for x in arguments))
    return step[0], white


def solution(mesh):
    in_specs = (
        P(None, ("row", "col")),
        P(None, ("row", "col")),
        P(None, ("row", "col")),
        P(None, ("row", "col")),
        P(("row", "col"), None),
        P(("row", "col"), None),
        P(),
    )
    out_specs = (P(), P(None, ("row", "col")))
    return jax.shard_map(body, mesh=mesh, in_specs=in_specs, out_specs=out_specs, check_vma=False)
```

```python
import functools
import math

import jax
import jax.numpy as jnp
from jax import lax
from jax.experimental import pallas as pl
from jax.experimental.pallas import tpu as pltpu
from jax.sharding import PartitionSpec as P

HIGH = lax.Precision.HIGHEST
ROOT_FIVE = math.sqrt(5.0)
NUGGET = 0.2
RANGE_BASE = (0.5, 0.5, 0.5, 0.5)
BLK = 128
PAN = 16
F32 = jnp.float32


def mm(a, b):
    return jnp.dot(a, b, precision=HIGH, preferred_element_type=F32)


def mm_tn(a, b):
    return lax.dot_general(
        a, b, (((0,), (0,)), ((), ())), precision=HIGH, preferred_element_type=F32
    )


def halves(x):
    high = x.astype(jnp.bfloat16)
    return high, (x - high.astype(F32)).astype(jnp.bfloat16)


def split_dot(a, b, dims):
    def dot(x, y):
        return lax.dot_general(x, y, (dims, ((), ())), preferred_element_type=F32)

    (ah, al), (bh, bl) = a, b
    return dot(ah, bh) + (dot(ah, bl) + dot(al, bh))


def mm3(a, b):
    return split_dot(halves(a), halves(b), ((1,), (0,)))


def mm3_tn(a, b):
    return split_dot(halves(a), halves(b), ((0,), (0,)))


def rows(b):
    return pl.ds(b * BLK, BLK)


def thirds(x):
    first = x.astype(jnp.bfloat16)
    rest = x - first.astype(F32)
    second = rest.astype(jnp.bfloat16)
    return first, second, (rest - second.astype(F32)).astype(jnp.bfloat16)


def outer_tn(x):
    a, b, c = thirds(x)
    left = jnp.concatenate([a, a, b, b, a, c], axis=0)[:, :BLK]
    right = jnp.concatenate([a, b, a, b, c, a], axis=0)
    return lax.dot_general(
        left, right, (((0,), (0,)), ((), ())), preferred_element_type=F32
    )


def six_wide(x):
    a, b, c = thirds(x)
    return jnp.concatenate([a, a, b, b, a, c], axis=1)


def six_deep(x):
    a, b, c = thirds(x)
    return jnp.concatenate([a, b, a, b, c, a], axis=0)


def spread_row(x, i):
    return jnp.broadcast_to(x[i : i + 1, :], (8, BLK))


def inverse_factor(s_ref):
    row8 = lax.broadcasted_iota(jnp.int32, (8, BLK), 0)
    panels = BLK // PAN
    own = PAN // 8
    va = [s_ref[g * 8 : g * 8 + 8, :BLK] for g in range(own)]
    vb = [s_ref[g * 8 : g * 8 + 8, BLK:] for g in range(own)]
    for p in range(panels):
        base = p * PAN
        groups = 2 * own if p + 1 < panels else own
        for g in range(own, groups):
            at = base + g * 8
            va.append(s_ref[at : at + 8, :BLK])
            vb.append(s_ref[at : at + 8, BLK:])
        cols = [
            [
                jnp.broadcast_to(va[g][:, base + j : base + j + 1], (8, BLK)) if g >= j // 8 else None
                for g in range(groups)
            ]
            for j in range(PAN)
        ]
        pivots = [jnp.ones((8, BLK), F32)] * own
        for k in range(PAN):
            gk, kk = divmod(k, 8)
            pivot = spread_row(cols[k][gk], kk)
            pivots[gk] = jnp.where(row8 == kk, pivot, pivots[gk])
            inv = 1.0 / pivot
            low = [cols[k][g] * inv if g >= gk else None for g in range(groups)]
            low[gk] = jnp.where(row8 > kk, low[gk], 0.0)
            for j in range(k + 1, PAN):
                other = spread_row(cols[k][j // 8], j % 8)
                for g in range(j // 8, groups):
                    cols[j][g] = cols[j][g] - low[g] * other
            xa, xb = spread_row(va[gk], kk), spread_row(vb[gk], kk)
            for g in range(gk, groups):
                va[g] = va[g] - low[g] * xa
                vb[g] = vb[g] - low[g] * xb
        for g in range(own):
            unit = lax.rsqrt(pivots[g])
            va[g] = va[g] * unit
            vb[g] = vb[g] * unit
            s_ref[base + g * 8 : base + g * 8 + 8, BLK:] = vb[g]
        done = base + 2 * PAN
        if done < BLK:
            top = jnp.concatenate(
                [jnp.concatenate(va[:own], axis=0), jnp.concatenate(vb[:own], axis=0)], axis=1
            )
            s_ref[done:, :] -= outer_tn(top)[done:, :]
        va, vb = va[own:], vb[own:]


def dot(a, b, dims=((1,), (0,))):
    return lax.dot_general(a, b, (dims, ((), ())), preferred_element_type=F32)


def beside(pair):
    return jnp.concatenate(pair, axis=1)


def folded(x):
    half = x.shape[1] // 2
    return x[:, :half] + x[:, half:]


def mm3_wide(a, b):
    (ah, al), (bh, bl) = a, b
    return folded(dot(ah, beside((bh, bl)))) + dot(al, bh)


MESH = pl.DeviceIdType.MESH


def onehot(index, count):
    return (lax.broadcasted_iota(jnp.int32, (count, index.shape[1]), 0) == index).astype(F32)


def onehot_rows(index, count):
    column = jnp.broadcast_to(index, (8, index.shape[1])).T[:, :1]
    return (lax.broadcasted_iota(jnp.int32, (index.shape[1], count), 1) == column).astype(F32)


def fused_kernel(
    per_tile, params, coords, ccoords, cidx, fidx, values, coarse, step_ref, white_ref,
    u_ref, li_ref, lt_ref, wt_ref, h_ref, z_ref, c_ref, s_ref, xr, xc, m_ref, pay, near, ccv, ccrow, ccrows,
    lp, cbuf, fbuf, hot_ref, pick_ref, own, upper, left, allc, term, terms, local_sem, send_sem, recv_sem,
):
    n_row, n_col = lax.axis_size("row"), lax.axis_size("col")
    count = n_row * n_col
    row, col = lax.axis_index("row"), lax.axis_index("col")
    me = row * n_col + col
    reps = values.shape[0]
    n = xr.shape[1]
    nb = n // BLK
    lead = n - BLK
    lb = nb - 1
    nc = cidx.shape[1]
    half = fidx.shape[1] // 2

    def place(d):
        other = lax.rem(me + d, count)
        return {"row": other // n_col, "col": lax.rem(other, n_col)}

    barrier = pltpu.get_barrier_semaphore()

    def greet(d, carry):
        pl.semaphore_signal(barrier, inc=1, device_id=place(d), device_id_type=MESH)
        return carry

    def fetch(src, dst, k):
        return pltpu.make_async_copy(src, dst, local_sem.at[k])

    early = [
        fetch(coords, pay.at[pl.ds(0, 4)], 0), fetch(ccoords, ccv, 1),
        fetch(cidx, cbuf, 2), fetch(fidx, fbuf, 3), fetch(params, lp, 6),
    ]
    late = [
        fetch(values, own, 4), fetch(coarse, allc.at[pl.ds(me * per_tile, per_tile)], 5),
    ]
    for each in early:
        each.start()
    lax.fori_loop(1, count, greet, 0)
    pay[4:, :] = jnp.zeros((4, BLK), F32)
    early[0].wait()
    early[1].wait()
    small = ccv[...]
    line = jnp.zeros((1, BLK), F32)
    wide = jnp.concatenate([small, jnp.zeros((4, BLK - per_tile), F32)], axis=1)
    for k in range(4):
        part = wide[k : k + 1, :]
        line = line + (pltpu.roll(part, k * per_tile, 1) if k else part)
    ccrow[...] = line
    ccrows[pl.ds(me, 1), :] = line
    pl.semaphore_wait(barrier, count - 1)

    def send(src, dst, k, where):
        return pltpu.make_async_remote_copy(
            src_ref=src, dst_ref=dst, send_sem=send_sem.at[k], recv_sem=recv_sem.at[k],
            device_id=where, device_id_type=MESH,
        )

    def push(src, dst, k):
        for dc in sorted(range(n_col), key=lambda d: -min(d, n_col - d)):

            def step(dr, carry, dc=dc):
                there = {"row": lax.rem(row + dr, n_row), "col": lax.rem(col + dc, n_col)}
                send(src, dst, k, there).start()
                return carry

            lax.fori_loop(0 if dc else 1, n_row, step, 0)

    def landed(ref, k):
        pltpu.make_async_copy(ref, ref, recv_sem.at[k]).wait()

    def left_here(ref, k):
        pltpu.make_async_copy(ref, ref, send_sem.at[k]).wait()

    down = {"row": lax.rem(row + 1, n_row)}
    across = {"col": lax.rem(col + 1, n_col)}
    push(ccrow, ccrows.at[pl.ds(me, 1)], 0)
    near_down = send(pay, near.at[0], 1, down)
    near_across = send(pay, near.at[1], 2, across)
    near_down.start()
    near_across.start()
    early[4].wait()
    row8 = lax.broadcasted_iota(jnp.int32, (8, BLK), 0)
    spread = jnp.zeros((8, BLK), F32)
    for k in range(4):
        spread = jnp.where(row8 == k, lp[1 + k], spread)
    base = jnp.ones((8, BLK), F32)
    for k in range(4):
        base = jnp.where(row8 == k, RANGE_BASE[k], base)
    scale = (1.0 / (jnp.exp(spread) * base))[:, :1]
    variance = jnp.exp(jnp.full((1, BLK), lp[0], F32))[:, :1]
    nugget = (NUGGET * jnp.exp(jnp.full((1, BLK), lp[5], F32)))[:, :1]
    alive = jnp.where(row > 0, 1.0, 0.0)

    early[2].wait()
    early[3].wait()
    wanted = cbuf[...]
    tile = wanted // per_tile
    slot = wanted - tile * per_tile
    hot_t = onehot(tile, count)
    hot_s = onehot(slot, per_tile)
    pick_u = onehot(fbuf[:, :half], BLK)
    pick_l = onehot(fbuf[:, half:], BLK)
    hot_ref[...] = onehot_rows(wanted, count * per_tile).astype(jnp.bfloat16)
    pick_ref[:half, :] = (onehot_rows(fbuf[:, :half], BLK) * alive).astype(jnp.bfloat16)
    pick_ref[half:, :] = onehot_rows(fbuf[:, half:], BLK).astype(jnp.bfloat16)

    near_down.wait_recv()
    near_across.wait_recv()
    xr[:, nc : nc + half] = mm(near[0], pick_u) * (scale * alive)
    xr[:, nc + half : lead] = mm(near[1], pick_l) * scale
    xr[:, lead:] = pay[...] * scale
    landed(ccrows.at[pl.ds(0, count - 1)], 0)
    for each in late:
        each.start()
    field_down = send(values, upper, 3, down)
    field_across = send(values, left, 4, across)
    mine = allc.at[pl.ds(me * per_tile, per_tile)]
    for dc in sorted(range(1, n_col), key=lambda d: -min(d, n_col - d)):
        send(coarse, mine, 5, {"col": lax.rem(col + dc, n_col)}).start()

    lines = mm_tn(ccrows[...], hot_t)
    for k in range(4):
        part = lines[k * per_tile : (k + 1) * per_tile, :] * hot_s
        xr[k : k + 1, :nc] = jnp.sum(part, axis=0, keepdims=True) * scale[k : k + 1, :]
    xr[5:, :nc] = jnp.zeros((3, nc), F32)
    point = lax.broadcasted_iota(jnp.int32, (1, n), 1)
    xr[4:5, :] = jnp.where((point >= nc) & (point < nc + half), alive, 1.0)
    for b in range(nb):
        xc[rows(b), :] = xr[:, b * BLK : (b + 1) * BLK].T

    def cover(r, carry):
        start = pl.multiple_of(r * 128, 128)
        here = pl.ds(start, 128)
        total = None
        for k in range(4):
            diff = xc[here, k : k + 1] - xr[k : k + 1, :]
            total = diff * diff if total is None else total + diff * diff
        live_c = xc[here, 4:5]
        paired = live_c * xr[4:5, :]
        root = ROOT_FIVE * jnp.sqrt(total)
        decay = jnp.exp(-root) * (variance * paired)
        ident = (
            lax.broadcasted_iota(jnp.int32, (128, n), 0) + start
            == lax.broadcasted_iota(jnp.int32, (128, n), 1)
        )
        u_ref[here, :] = (1.0 + root + root * root / 3.0) * decay + jnp.where(
            ident, live_c * nugget + 1.0 - live_c, 0.0
        )
        c_ref[here, :] = (5.0 / 3.0) * (1.0 + root) * decay
        return carry

    lax.fori_loop(0, n // 128, cover, 0)

    eye = (
        lax.broadcasted_iota(jnp.int32, (BLK, BLK), 0)
        == lax.broadcasted_iota(jnp.int32, (BLK, BLK), 1)
    ).astype(F32)
    def band(line):
        return allc.at[pl.ds(line * (n_col * per_tile), n_col * per_tile)]

    pair = n_row // 2
    sibling = {"row": row + 1 - 2 * lax.rem(row, 2)}
    for b in range(nb):
        s_ref[:, :BLK] = u_ref[rows(b), b * BLK : (b + 1) * BLK]
        s_ref[:, BLK:] = eye
        inverse_factor(s_ref)
        inv = s_ref[:, BLK:]
        if b == 1:
            late[1].wait()
            landed(allc.at[pl.ds(0, (n_col - 1) * per_tile)], 5)
            for k in range(1, pair):
                send(band(row), band(row), 7, {"row": lax.rem(row + 2 * k, n_row)}).start()
            field_down.start()
            field_across.start()
        if b == lb:
            break
        here, rest = b * BLK, (b + 1) * BLK
        along = dot(six_wide(inv), six_deep(u_ref[rows(b), rest:]))
        u_ref[rows(b), rest:] = along
        tall, flat = six_wide(along.T), six_deep(along)
        for i in range(b + 1, nb):
            at = i * BLK - rest
            u_ref[rows(i), i * BLK :] -= dot(tall[at : at + BLK, :], flat[:, at:])
        li_ref[rows(b), here:rest] = inv
        lt_ref[rows(b), here:rest] = inv.T
        if b:
            above = mm_tn(u_ref[:here, here:rest], li_ref[:here, :here])
            side = -dot(six_wide(inv), six_deep(above))
            li_ref[rows(b), :here] = side
            for i in range(b):
                lt_ref[rows(i), here:rest] = side[:, i * BLK : (i + 1) * BLK].T
                li_ref[rows(i), here:rest] = jnp.zeros((BLK, BLK), F32)
                lt_ref[rows(b), i * BLK : (i + 1) * BLK] = jnp.zeros((BLK, BLK), F32)

    turned = inv.T
    wt_ref[lead:, :] = turned
    wt_ref[:lead, :] = -mm(lt_ref[...], mm(u_ref[:lead, lead:], turned))

    wt = halves(wt_ref[...])
    wide = beside(wt)

    def slopes(r, carry):
        here = pl.ds(pl.multiple_of(r * BLK, BLK), BLK)
        for k in range(4):
            diff = xc[here, k : k + 1] - xr[k : k + 1, :]
            high, low = halves(c_ref[here, :] * (diff * diff))
            h_ref[here, k * BLK : (k + 1) * BLK] = folded(dot(high, wide)) + dot(low, wt[0])
        h_ref[here, 4 * BLK :] = nugget * wt_ref[here, :]
        return carry

    lax.fori_loop(0, nb, slopes, 0)
    landed(allc.at[pl.ds(0, (pair - 1) * n_col * per_tile)], 7)
    for k in range(pair):
        line = lax.rem(row + 2 * k, n_row)
        send(band(line), band(line), 8, sibling).start()
    z_ref[...] = split_dot(wt, halves(h_ref[...]), ((0,), (0,)))
    lower = halves(li_ref[...])
    mid = lb // 2 * BLK
    whole = halves(h_ref[:lead, :])
    h_ref[mid:lead, :] = split_dot([x[mid:, :] for x in lower], whole, ((1,), (0,)))
    h_ref[:mid, :] = split_dot(
        [x[:mid, :mid] for x in lower], [x[:mid, :] for x in whole], ((1,), (0,))
    )

    def h_of(i):
        i = 4 if i in (0, 5) else i - 1
        return h_ref[:lead, i * BLK : (i + 1) * BLK]

    def z_of(i):
        if i == 0:
            return eye - z_ref[:, 4 * BLK :]
        return z_ref[:, (i - 1) * BLK : i * BLK]

    lane1 = lax.broadcasted_iota(jnp.int32, (1, BLK), 1)
    out = jnp.zeros((1, BLK), F32)
    spot = 0
    for i in range(6):
        for j in range(i, 6):
            sign = -2.0 if (i == 0) != (j == 0) else 2.0
            both = sign * jnp.sum(h_of(i) * h_of(j), axis=0, keepdims=True)
            both = both + jnp.sum(z_of(i) * z_of(j), axis=0, keepdims=True)
            value = (0.5 * reps) * jnp.sum(both, axis=1, keepdims=True)
            out = out + jnp.where(lane1 == spot, value, 0.0)
            spot += 1


    left_here(ccrows.at[pl.ds(0, count - 1)], 0)
    near_down.wait_send()
    near_across.wait_send()
    late[0].wait()
    field_down.wait()
    field_across.wait()
    left_here(allc.at[pl.ds(0, (n_col - 1) * per_tile)], 5)
    left_here(allc.at[pl.ds(0, (pair - 1) * n_col * per_tile)], 7)
    landed(allc.at[pl.ds(0, pair * n_col * per_tile)], 8)
    left_here(allc.at[pl.ds(0, pair * n_col * per_tile)], 8)

    hot_c = hot_ref[...]
    pick = pick_ref[...]
    coarse_wide = dot(hot_c, wide[:nc, :], ((0,), (0,))).astype(jnp.bfloat16)
    high, low = halves(allc[...])
    both = dot(coarse_wide, high, ((0,), (0,)))
    white = (both[:BLK, :] + both[BLK:, :] + dot(coarse_wide[:, :BLK], low, ((0,), (0,)))).T
    near_wide = jnp.concatenate(
        [
            dot(pick[:half, :], wide[nc : nc + half, :], ((0,), (0,))).astype(jnp.bfloat16),
            dot(pick[half:, :], wide[nc + half : lead, :], ((0,), (0,))).astype(jnp.bfloat16),
            wide[lead:, :],
        ],
        axis=0,
    )
    fields = halves(jnp.concatenate([upper[...], left[...], own[...]], axis=1))
    white = white + folded(dot(fields[0], near_wide)) + dot(fields[1], near_wide[:, :BLK])
    white_ref[...] = white
    parts = halves(white)
    white_wide = beside(parts)
    seen = folded(dot(high, white_wide)) + dot(low, parts[0])
    m_ref[:nc, :] = folded(dot(hot_c, beside(halves(seen))))
    seen = folded(dot(fields[0][:, : 2 * BLK], white_wide, ((0,), (0,)))) + dot(
        fields[1][:, : 2 * BLK], parts[0], ((0,), (0,))
    )
    seen = beside(halves(seen))
    m_ref[nc : nc + half, :] = folded(dot(pick[:half, :], seen[:BLK, :]))
    m_ref[nc + half :, :] = folded(dot(pick[half:, :], seen[BLK:, :]))
    m_ref[...] = mm3_wide(lower, halves(m_ref[...]))
    gram = mm3_tn(white, white)
    weight = 0.5 * gram - (0.5 * reps) * eye
    for i in range(6):
        at = 4 if i in (0, 5) else i - 1
        lead_part = jnp.sum(m_ref[...] * h_ref[:lead, at * BLK : (at + 1) * BLK], axis=0, keepdims=True)
        z = z_ref[:, at * BLK : (at + 1) * BLK]
        if i == 0:
            z = eye - z
            lead_part = -lead_part
        both = lead_part + jnp.sum(weight * z, axis=0, keepdims=True)
        value = jnp.sum(both, axis=1, keepdims=True)
        out = out + jnp.where(lane1 == 21 + i, value, 0.0)

    term[...] = out
    terms[pl.ds(me, 1), :] = out
    push(term, terms.at[pl.ds(me, 1)], 6)
    landed(terms.at[pl.ds(0, count - 1)], 6)
    total = jnp.sum(terms[...], axis=0, keepdims=True)
    cell = {}
    spot = 0
    for i in range(6):
        for j in range(i, 6):
            cell[i, j] = total[:, spot : spot + 1]
            spot += 1
    right_side = [total[:, 21 + i : 22 + i] for i in range(6)]
    for k in range(6):
        inv = 1.0 / cell[k, k]
        for i in range(k + 1, 6):
            ratio = cell[k, i] * inv
            for j in range(i, 6):
                cell[i, j] = cell[i, j] - ratio * cell[k, j]
            right_side[i] = right_side[i] - ratio * right_side[k]
    for k in range(5, -1, -1):
        acc = right_side[k]
        for j in range(k + 1, 6):
            acc = acc - cell[k, j] * right_side[j]
        right_side[k] = acc / cell[k, k]
    result = jnp.zeros((1, BLK), F32)
    for i in range(6):
        result = jnp.where(lane1 == i, right_side[i], result)
    step_ref[...] = result[:, :6]
    left_here(terms.at[pl.ds(0, count - 1)], 6)


def shape(*dims):
    return jax.ShapeDtypeStruct(dims, F32)


def body(coords, values, coarse_coords, coarse_values, fine_index, coarse_index, log_params):
    half = fine_index.shape[1] // 2
    reps, block = values.shape
    nc = coarse_index.shape[1]
    per_tile = coarse_coords.shape[1]
    n = nc + 2 * half + block
    lead = n - block
    count = lax.axis_size("row") * lax.axis_size("col")
    anywhere = pl.BlockSpec(memory_space=pl.ANY)
    inner = pl.BlockSpec(memory_space=pltpu.VMEM)
    arguments = (
        log_params, coords, coarse_coords, coarse_index, fine_index, values, coarse_values.T
    )
    step, white = pl.pallas_call(
        functools.partial(fused_kernel, per_tile),
        out_shape=[shape(1, 6), shape(reps, block)],
        in_specs=[anywhere] * len(arguments),
        out_specs=[inner, inner],
        scratch_shapes=[
            pltpu.VMEM((n, n), F32), pltpu.VMEM((lead, lead), F32), pltpu.VMEM((lead, lead), F32),
            pltpu.VMEM((n, BLK), F32),
            pltpu.VMEM((n, 5 * BLK), F32), pltpu.VMEM((BLK, 5 * BLK), F32),
            pltpu.VMEM((n, n), F32), pltpu.VMEM((BLK, 2 * BLK), F32),
            pltpu.VMEM((8, n), F32), pltpu.VMEM((n, 8), F32), pltpu.VMEM((lead, BLK), F32),
            pltpu.VMEM((8, BLK), F32), pltpu.VMEM((2, 8, BLK), F32), pltpu.VMEM((4, per_tile), F32),
            pltpu.VMEM((1, BLK), F32), pltpu.VMEM((count, BLK), F32),
            pltpu.SMEM((6,), F32), pltpu.VMEM((1, nc), jnp.int32), pltpu.VMEM((1, 2 * half), jnp.int32),
            pltpu.VMEM((nc, count * per_tile), jnp.bfloat16),
            pltpu.VMEM((2 * half, BLK), jnp.bfloat16),
            pltpu.VMEM((reps, block), F32), pltpu.VMEM((reps, block), F32),
            pltpu.VMEM((reps, block), F32), pltpu.VMEM((count * per_tile, reps), F32),
            pltpu.VMEM((1, BLK), F32), pltpu.VMEM((count, BLK), F32),
            pltpu.SemaphoreType.DMA((7,)), pltpu.SemaphoreType.DMA((9,)),
            pltpu.SemaphoreType.DMA((9,)),
        ],
        compiler_params=pltpu.CompilerParams(
            collective_id=0, has_side_effects=True, vmem_limit_bytes=40 * 1024 * 1024
        ),
    )(*(pltpu.with_memory_space_constraint(x, pltpu.HBM) for x in arguments))
    return step[0], white


def solution(mesh):
    in_specs = (
        P(None, ("row", "col")),
        P(None, ("row", "col")),
        P(None, ("row", "col")),
        P(None, ("row", "col")),
        P(("row", "col"), None),
        P(("row", "col"), None),
        P(),
    )
    out_specs = (P(), P(None, ("row", "col")))
    return jax.shard_map(body, mesh=mesh, in_specs=in_specs, out_specs=out_specs, check_vma=False)
```
